32 devices in a mesh: row: 4 (over y, core), col: 8 (over z, x).
Axes of the slice: x: 2, y: 2, z: 4, core: 2. Of those that a mesh axis runs over, the one named last changes fastest.
Arguments:
- coarse_feats: bfloat16 [8192, 512], P(('row', 'col')), may hold values from -6 to 6
- fine_feats: bfloat16 [32768, 256], P(('row', 'col')), may hold values from -6 to 6
- parent_index: int32 [32768], P(('row', 'col')), may hold values from 0 to 8191, as said below
- nbr_offset: int32 [27, 32768], P(None, ('row', 'col')), may hold values from -256 to 257, as said below
- z_position: int32 [32768], P(('row', 'col')), may hold values from 0 to 32767, as said below
- segment_id: int32 [32768], P(('row', 'col')), may hold values from 0 to 63, never falling along the last dimension, each value on 1 to 2048 neighbouring positions
- w_parent: bfloat16 [512, 256], replicated, may hold values from -0.25 to 0.25
- w_skip: bfloat16 [256, 256], replicated, may hold values from -0.375 to 0.375
- conv_taps: float32 [27, 256], replicated, may hold values from -1.5 to 1.5
- w_cpe: bfloat16 [256, 256], replicated, may hold values from -0.375 to 0.375
- w_qkv: bfloat16 [256, 768], replicated
- w_out: bfloat16 [256, 256], replicated, may hold values from -0.375 to 0.375
- w_up: bfloat16 [256, 1024], replicated, may hold values from -0.375 to 0.375
- w_down: bfloat16 [1024, 256], replicated, may hold values from -0.1875 to 0.1875
- w_cls: bfloat16 [13, 256], replicated, may hold values from -0.375 to 0.375
Outputs:
- logits: float32 [13, 32768], P(None, ('row', 'col'))
The draws below stay inside these ranges and needn't reach their ends.
Inputs may be any that keep to these rules, and one draw needn't show every extreme that they name: parent_index[g] differs from g // 4 by at most 128; it is that far below at the first point of every device's shard and that far above at the last, where the grid allows. `nbr_offset`: the offset for kernel position 13 is 0; present neighbours lie inside the grid; the first kernel offset of each shard's first point is -256 and the last offset of each shard's last point is 256, where the grid allows. `z_position`: a permutation; at most 64 of one device's 1024 points have z positions in one device's block of 1024 consecutive z positions, and exactly 64 for some pairs of devices.
All inputs are finite; a program needn't handle non-finite values.
Results may differ from the reference program's by a relative error of at most 0.014.
The reference program's roundings to bfloat16 on the way count: a program that leaves them out, or rounds other values in their place, can miss the bound.
Values may be sent and summed in bfloat16 or wider, within the bound.
A program may use at most 64 MiB of HBM per device.

```python
import math
import jax
import jax.numpy as jnp
import numpy as np
from jax import lax

D = 256
DC = 512
HEADS = 16
HID = 1024
CLASSES = 13
TAPS = 27
PATCH = 1024
FINE_DEV = 1024
COARSE_DEV = 256
REACH = 256
FINE = 32768
COARSE = 8192
HEAD_DIM = 16
DEVICES = 32


def draw_parent_index(key, part):
    points = jnp.arange(FINE, dtype=jnp.int32)
    half_span = COARSE_DEV // 2
    offsets = jax.random.randint(key, (FINE,), -half_span, half_span + 1, dtype=jnp.int32)
    local_row = points % FINE_DEV
    offsets = jnp.where(local_row == 0, -half_span, offsets)
    offsets = jnp.where(local_row == FINE_DEV - 1, half_span, offsets)
    return jnp.clip(points // 4 + offsets, 0, COARSE - 1).astype(jnp.int32)


def draw_nbr_offset(key, part):
    first_key = jax.random.fold_in(key, 11)
    second_key = jax.random.fold_in(key, 12)
    points = jnp.arange(FINE, dtype=jnp.int32)[None, :]
    tap_ids = jnp.arange(TAPS, dtype=jnp.int32)[:, None]
    offsets = jax.random.randint(first_key, (TAPS, FINE), -REACH, REACH + 1, dtype=jnp.int32)
    missing = jax.random.randint(second_key, (TAPS, FINE), 0, 3, dtype=jnp.int32) == 0
    offsets = jnp.where(missing, REACH + 1, offsets)
    offsets = jnp.where(tap_ids == TAPS // 2, 0, offsets)
    local_row = points % FINE_DEV
    offsets = jnp.where((tap_ids == 0) & (local_row == 0), -REACH, offsets)
    offsets = jnp.where((tap_ids == TAPS - 1) & (local_row == FINE_DEV - 1), REACH, offsets)
    target = points + offsets
    outside = (offsets != REACH + 1) & ((target < 0) | (target >= FINE))
    return jnp.where(outside, REACH + 1, offsets).astype(jnp.int32)


def draw_z_position(key, part):
    count = DEVICES
    share = FINE_DEV // DEVICES
    level_key = jax.random.fold_in(key, 21)
    source_key = jax.random.fold_in(key, 22)
    target_key = jax.random.fold_in(key, 23)
    levels = jnp.concatenate([jnp.full((count // 4,), 2 * share, jnp.int32), jnp.full((count // 2,), share, jnp.int32), jnp.zeros((count - count // 4 - count // 2,), jnp.int32)])
    weights = jax.random.permutation(level_key, levels)
    segment_ends = jnp.cumsum(weights)
    slot_ids = jnp.arange(FINE_DEV, dtype=jnp.int32)
    shift_of_slot = jnp.sum((slot_ids[:, None] >= segment_ends[None, :]).astype(jnp.int32), axis=1)
    device_ids = jnp.arange(count, dtype=jnp.int32)
    source_perm = jax.vmap(lambda dev_id: jax.random.permutation(jax.random.fold_in(source_key, dev_id), FINE_DEV))(device_ids).astype(jnp.int32)
    target_perm = jax.vmap(lambda dev_id: jax.random.permutation(jax.random.fold_in(target_key, dev_id), FINE_DEV))(device_ids).astype(jnp.int32)
    dest_dev = (device_ids[:, None] + shift_of_slot[None, :]) % count
    z_values = dest_dev * FINE_DEV + target_perm[dest_dev, slot_ids[None, :]]
    hilbert_rows = device_ids[:, None] * FINE_DEV + source_perm
    return jnp.zeros((FINE,), jnp.int32).at[hilbert_rows.reshape(-1)].set(z_values.reshape(-1).astype(jnp.int32))


def draw_w_qkv(key, part):
    base = jax.random.normal(key, (D, 3 * D), jnp.float32) * D ** (-0.5)
    return base.astype(jnp.bfloat16)


def shard_levels(stream_key, extent, pieces, smallest, largest):
    def one(position, blocks):
        heights = jax.random.uniform(jax.random.fold_in(jax.random.fold_in(stream_key, 6), position), (blocks,), jnp.float32, smallest / len(pieces), largest / len(pieces))
        return jnp.repeat(jnp.exp(heights), extent[position] // blocks).reshape((-1,) + (1,) * (len(extent) - position - 1))

    gain = one(*pieces[0])
    for cut in pieces[1:]:
        gain = gain * one(*cut)
    return gain


def length_profile(amount, total, limit, slope):
    loads = [(1 << 20) // math.isqrt(grade ** slope) + 1 for grade in range(2, amount + 1)]
    surplus, holding = total - limit - (amount - 1), [1] * (amount - 1)
    while surplus > 0:
        candidates = [i for i in range(amount - 1) if holding[i] < limit]
        mass, remaining = sum([loads[i] for i in candidates]), surplus
        for i in candidates:
            addition = min(limit - holding[i], max(1, remaining * loads[i] // mass), surplus)
            holding[i] = holding[i] + addition
            surplus = surplus - addition
    return np.array([limit] + holding)


def ragged_sizes(key, number_of, total, reach, lean):
    if number_of == 2:
        one = jax.random.randint(key, (), max(1, total - reach), min(reach, total - 1) + 1)
        return jnp.stack([one, total - one])
    sizes = jnp.asarray(length_profile(number_of, total, reach, lean), jnp.int32)
    twos = (number_of - 1) // 2
    source_of, receiver = sizes[1:1 + 2 * twos:2], sizes[2:2 + 2 * twos:2]
    slack = jnp.minimum(source_of - 1, reach - receiver)
    moved = jax.random.randint(jax.random.fold_in(key, 1), (twos,), 0, 1 << 20) % (slack + 1)
    sizes = sizes.at[1:1 + 2 * twos:2].set(source_of - moved).at[2:2 + 2 * twos:2].set(receiver + moved)
    return sizes[jax.random.permutation(jax.random.fold_in(key, 2), number_of)]


def bell_draw(rng, extent, scale, reach, shards=(), held_as=jnp.bfloat16):
    entries = jax.random.normal(rng, extent, jnp.float32) * scale
    if len(shards) > 0:
        entries = shard_levels(rng, extent, shards, -0.22, 0.18) * entries
    return jnp.clip(entries, min=-reach, max=reach).astype(held_as)


def setup_inputs(seed: int = 0) -> dict:
    arg_keys = jax.random.split(jax.random.key(seed), 16)
    coarse_feats = bell_draw(arg_keys[0], (COARSE, DC), 1.0, 6.0, ((0, 32),))
    fine_feats = bell_draw(arg_keys[1], (FINE, D), 1.0, 6.0, ((0, 32),))
    parent_index = draw_parent_index(jax.random.fold_in(arg_keys[15], 71), 0)
    nbr_offset = draw_nbr_offset(jax.random.fold_in(arg_keys[15], 71), 0)
    z_position = draw_z_position(jax.random.fold_in(arg_keys[15], 71), 0)
    segment_id = jnp.searchsorted(jnp.cumsum(ragged_sizes(arg_keys[5], FINE // 512, FINE, 2048, 2)), jnp.arange(FINE), side="right").astype(jnp.int32)
    w_parent = bell_draw(arg_keys[6], (DC, D), DC ** -0.5, 0.25)
    w_skip = bell_draw(arg_keys[7], (D, D), D ** -0.5, 0.375)
    conv_taps = bell_draw(arg_keys[8], (TAPS, D), 0.25, 1.5, (), jnp.float32)
    w_cpe = bell_draw(arg_keys[9], (D, D), D ** -0.5, 0.375)
    w_qkv = draw_w_qkv(jax.random.fold_in(arg_keys[15], 71), 0)
    w_out = bell_draw(arg_keys[11], (D, D), D ** -0.5, 0.375)
    w_up = bell_draw(arg_keys[12], (D, HID), D ** -0.5, 0.375)
    w_down = bell_draw(arg_keys[13], (HID, D), HID ** -0.5, 0.1875)
    w_cls = bell_draw(arg_keys[14], (CLASSES, D), D ** -0.5, 0.375)
    return {"coarse_feats": coarse_feats, "fine_feats": fine_feats, "parent_index": parent_index, "nbr_offset": nbr_offset, "z_position": z_position, "segment_id": segment_id, "w_parent": w_parent, "w_skip": w_skip, "conv_taps": conv_taps, "w_cpe": w_cpe, "w_qkv": w_qkv, "w_out": w_out, "w_up": w_up, "w_down": w_down, "w_cls": w_cls}


def layer_norm(values):
    center = values - lax.optimization_barrier(jnp.mean(values, axis=-1, keepdims=True))
    spread = lax.optimization_barrier(jnp.mean(center * center, axis=-1, keepdims=True))
    return center * lax.rsqrt(spread + 1e-05)

def attend_all(z_feats, segment_id, w_qkv, w_out):
    normed = layer_norm(z_feats.astype(jnp.float32)).astype(jnp.bfloat16)
    qkv_all = jnp.dot(normed, w_qkv, preferred_element_type=jnp.float32).astype(jnp.bfloat16)
    scale_factor = HEAD_DIM ** (-0.5)

    def one_patch(start):
        block = lax.dynamic_slice_in_dim(qkv_all, start, PATCH, 0).astype(jnp.float32)
        seg_block = lax.dynamic_slice_in_dim(segment_id, start, PATCH, 0)
        same_seg = seg_block[:, None] == seg_block[None, :]
        split = block.reshape(PATCH, 3, HEADS, HEAD_DIM)
        scores = jnp.einsum('qhd,khd->hqk', split[:, 0], split[:, 1]) * scale_factor
        scores = jnp.where(same_seg[None], scores, -1e+30)
        row_max = lax.optimization_barrier(jnp.max(scores, axis=-1, keepdims=True))
        exp_scores = jnp.exp(scores - row_max)
        probs = (exp_scores / lax.optimization_barrier(jnp.sum(exp_scores, axis=-1, keepdims=True))).astype(jnp.bfloat16)
        out_heads = jnp.einsum('hqk,khd->qhd', probs.astype(jnp.float32), split[:, 2])
        return out_heads.reshape(PATCH, D).astype(jnp.bfloat16)
    starts = (jnp.arange(FINE // PATCH) * PATCH).astype(jnp.int32)
    att = lax.map(one_patch, starts).reshape(FINE, D)
    return jnp.dot(att, w_out, preferred_element_type=jnp.float32).astype(jnp.bfloat16)

def reference(coarse_feats, fine_feats, parent_index, nbr_offset, z_position, segment_id, w_parent, w_skip, conv_taps, w_cpe, w_qkv, w_out, w_up, w_down, w_cls):
    parent = jax.nn.gelu(layer_norm(jnp.dot(coarse_feats, w_parent, preferred_element_type=jnp.float32))).astype(jnp.bfloat16)
    skip = jax.nn.gelu(layer_norm(jnp.dot(fine_feats, w_skip, preferred_element_type=jnp.float32)))
    feat = (parent[parent_index].astype(jnp.float32) + skip).astype(jnp.bfloat16)
    point_index = jnp.arange(FINE, dtype=jnp.int32)

    def add_tap(tap_index, running):
        offsets = nbr_offset[tap_index]
        present = offsets != REACH + 1
        source = jnp.where(present, point_index + offsets, 0).astype(jnp.int32)
        gathered = feat[source].astype(jnp.float32) * conv_taps[tap_index][None, :]
        return running + jnp.where(present[:, None], gathered, jnp.float32(0.0))
    conv = lax.fori_loop(0, TAPS, add_tap, jnp.zeros((FINE, D), jnp.float32)).astype(jnp.bfloat16)
    x_feats = (feat.astype(jnp.float32) + layer_norm(jnp.dot(conv, w_cpe, preferred_element_type=jnp.float32))).astype(jnp.bfloat16)
    z_feats = jnp.zeros_like(x_feats).at[z_position].set(x_feats)
    att_out = attend_all(z_feats, segment_id, w_qkv, w_out)
    x_two = x_feats.astype(jnp.float32) + att_out[z_position].astype(jnp.float32)
    hidden = jax.nn.gelu(jnp.dot(layer_norm(x_two).astype(jnp.bfloat16), w_up, preferred_element_type=jnp.float32)).astype(jnp.bfloat16)
    x_three = x_two + jnp.dot(hidden, w_down, preferred_element_type=jnp.float32)
    final_norm = layer_norm(x_three).astype(jnp.bfloat16)
    return jnp.dot(w_cls, final_norm.T, preferred_element_type=jnp.float32)
```

```python
import functools
import math

import jax
import jax.numpy as jnp
from jax import lax
from jax.experimental import pallas as pl
from jax.experimental.pallas import tpu as pltpu
from jax.sharding import PartitionSpec as P

HEADS = 16
PATCH = 1024
REACH = 256
AXES = ("row", "col")
BF = jnp.bfloat16
F32 = jnp.float32
I32 = jnp.int32
VM = pl.BlockSpec(memory_space=pltpu.VMEM)


def dot(a, b):
    return jnp.dot(a, b, preferred_element_type=F32)


def dot_nt(a, b):
    return lax.dot_general(a, b, (((1,), (1,)), ((), ())), preferred_element_type=F32)


def layer_norm(values):
    center = values - jnp.mean(values, axis=-1, keepdims=True)
    spread = jnp.mean(center * center, axis=-1, keepdims=True)
    return center * lax.rsqrt(spread + 1e-05)


def pick(index, rows, cols, dim):
    grid = lax.broadcasted_iota(I32, (rows, cols), dim)
    return jnp.where(grid == index, 1.0, 0.0).astype(BF)


def column(row):
    return jnp.broadcast_to(row, (128, row.shape[1])).T[:, :1]


def place(device):
    inner = lax.axis_size("col")
    return (device // inner, device % inner)


def greet(me, devices):
    barrier = pltpu.get_barrier_semaphore()

    def signal(k, carry):
        pl.semaphore_signal(
            barrier, inc=1, device_id=place((me + k) % devices),
            device_id_type=pl.DeviceIdType.MESH,
        )
        return carry

    lax.fori_loop(1, devices, signal, 0)
    return lambda: pl.semaphore_wait(barrier, devices - 1)


def ship(src, dst, send_sem, recv_sem, device):
    return pltpu.make_async_remote_copy(
        src_ref=src, dst_ref=dst, send_sem=send_sem, recv_sem=recv_sem,
        device_id=place(device), device_id_type=pl.DeviceIdType.MESH,
    )


def spread(src_ref, dst_ref, send_sems, recv_sems, me, devices):
    def start(k, carry):
        peer = (me + k) % devices
        ship(
            src_ref.at[peer], dst_ref.at[me], send_sems.at[peer], recv_sems.at[me], peer
        ).start()
        return carry

    lax.fori_loop(1, devices, start, 0)


def gather_in(src_ref, dst_ref, send_sems, recv_sems, me, devices):
    def finish(k, carry):
        peer = (me + k) % devices
        ship(
            src_ref.at[peer], dst_ref.at[peer], send_sems.at[peer], recv_sems.at[peer], peer
        ).wait()
        return carry

    lax.fori_loop(1, devices, finish, 0)


def encode_kernel(
    devices, capacity, margin,
    z_ref, coarse_ref, fine_ref, parent_ref, nbr_ref,
    w_parent_ref, w_skip_ref, taps_ref, w_cpe_ref,
    pos_ref, got_ref, recv_ref,
    x_ref, slot_ref, take_ref, par_ref, edge_ref, edge_parent_ref, skip_ref, feat_ref, send_ref,
    send_sems, recv_sems, feat_send_sems, feat_recv_sems, send_side, recv_side,
):
    me = lax.axis_index(AXES)
    entered = greet(me, devices)
    rows = z_ref.shape[1]
    coarse_rows = coarse_ref.shape[0]
    coarse = par_ref.shape[0]
    block = 256
    par_ref[margin : margin + coarse_rows, :] = jax.nn.gelu(
        layer_norm(dot(coarse_ref[...], w_parent_ref[...]))
    ).astype(BF)

    z = z_ref[...]
    dest = z // rows
    slot = z % rows
    onehot = pick(dest, devices, rows, 0)
    earlier = lax.broadcasted_iota(I32, (rows, rows), 0) < lax.broadcasted_iota(I32, (rows, rows), 1)
    ahead = dot(onehot, jnp.where(earlier, 1.0, 0.0).astype(BF))
    rank = jnp.sum(ahead * onehot.astype(F32), axis=0, keepdims=True).astype(I32)
    pos = dest * capacity + rank
    pos_ref[...] = pos

    entered()
    after, before = (me + 1) % devices, (me + devices - 1) % devices
    moves = [
        ship(
            par_ref.at[pl.ds(coarse_rows, margin), :], par_ref.at[pl.ds(0, margin), :],
            send_side.at[0], recv_side.at[0], after,
        ),
        ship(
            par_ref.at[pl.ds(margin, margin), :],
            par_ref.at[pl.ds(margin + coarse_rows, margin), :],
            send_side.at[1], recv_side.at[1], before,
        ),
        ship(
            parent_ref.at[:, pl.ds(rows - REACH, REACH)], edge_parent_ref.at[0],
            send_side.at[2], recv_side.at[2], after,
        ),
        ship(
            parent_ref.at[:, pl.ds(0, REACH)], edge_parent_ref.at[1],
            send_side.at[3], recv_side.at[3], before,
        ),
        ship(
            fine_ref.at[pl.ds(rows - REACH, REACH), :], edge_ref.at[0],
            send_side.at[4], recv_side.at[4], after,
        ),
        ship(
            fine_ref.at[pl.ds(0, REACH), :], edge_ref.at[1],
            send_side.at[5], recv_side.at[5], before,
        ),
    ]
    for move in moves:
        move.start()

    code = slot + 1
    part = lax.broadcasted_iota(I32, (16, rows), 0)
    digits = jnp.where(part == 0, code // 32, jnp.where(part == 1, code % 32, 0))
    digits = digits.astype(F32).astype(BF)
    total = devices * capacity
    step = min(512, total)
    for start in range(0, total, step):
        got = dot_nt(digits, pick(pos - start, step, rows, 0)).astype(I32)
        got = got[0:1] * 32 + got[1:2] - 1
        for d in range(step // capacity):
            slot_ref[start // capacity + d] = got[:, d * capacity : (d + 1) * capacity]
    spread(slot_ref, take_ref, send_sems, recv_sems, me, devices)
    take_ref[me] = slot_ref[me]

    def skips(i, carry):
        at = pl.ds(pl.multiple_of(i * block, block), block)
        skip_ref[at, :] = jax.nn.gelu(layer_norm(dot(fine_ref[at, :], w_skip_ref[...])))
        return carry

    lax.fori_loop(0, rows // block, skips, 0)
    base_row = me * coarse_rows - margin
    for move in moves:
        move.wait()

    for side, start in ((0, 0), (1, REACH + rows)):
        chosen = dot(
            pick(column(edge_parent_ref[side] - base_row), REACH, coarse, 1), par_ref[...]
        )
        skip = jax.nn.gelu(layer_norm(dot(edge_ref[side], w_skip_ref[...])))
        feat_ref[start : start + REACH, :] = (chosen + skip).astype(BF)

    def join(i, carry):
        base = pl.multiple_of(i * block, block)
        at = pl.ds(base, block)
        chosen = dot(pick(column(parent_ref[:, at] - base_row), block, coarse, 1), par_ref[...])
        feat_ref[pl.ds(base + REACH, block), :] = (chosen + skip_ref[at, :]).astype(BF)
        return carry

    lax.fori_loop(0, rows // block, join, 0)
    window = block + 2 * REACH

    def conv(i, carry):
        base = pl.multiple_of(i * block, block)
        at = pl.ds(base, block)
        cells = feat_ref[pl.ds(base, window), :]
        offsets = nbr_ref[:, at].T
        here = lax.broadcasted_iota(I32, offsets.shape, 0) + REACH
        source = jnp.where(offsets != REACH + 1, here + offsets, -1)
        acc = jnp.zeros((block, cells.shape[1]), F32)
        for t in range(nbr_ref.shape[0]):
            acc = acc + dot(pick(source[:, t : t + 1], block, window, 1), cells) * taps_ref[t : t + 1, :]
        out = layer_norm(dot(acc.astype(BF), w_cpe_ref[...]))
        center = feat_ref[pl.ds(base + REACH, block), :]
        x_ref[at, :] = (center.astype(F32) + out).astype(BF)
        return carry

    lax.fori_loop(0, rows // block, conv, 0)
    pos = pos_ref[...]
    per = block // capacity

    def pack(i, carry):
        sent = dot(pick(pos - i * block, block, rows, 0), x_ref[...]).astype(BF)
        send_ref[pl.ds(i * per, per)] = sent.reshape(per, capacity, sent.shape[1])
        return carry

    lax.fori_loop(0, devices // per, pack, 0)
    spread(send_ref, recv_ref, feat_send_sems, feat_recv_sems, me, devices)
    recv_ref[me] = send_ref[me]
    gather_in(slot_ref, take_ref, send_sems, recv_sems, me, devices)
    for d in range(devices):
        got_ref[:, d * capacity : (d + 1) * capacity] = take_ref[d]
    gather_in(send_ref, recv_ref, feat_send_sems, feat_recv_sems, me, devices)


def gelu(x):
    half = 0.5 * x
    return half + half * jnp.tanh(x * (0.7978845608028654 + 0.035677408136300125 * (x * x)))


def decode_kernel(
    devices, capacity, classes,
    recv_ref, slot_row_ref, seg_ref, pos_ref,
    w_qkv_ref, w_out_ref, w_up_ref, w_down_ref, w_cls_ref,
    out_ref,
    zx_ref, normed_ref, kx_ref, qh_ref, ql_ref, v_ref, fq_ref, s_ref, m_ref, att_ref,
    logit_ref, back_ref, ret_ref, home_ref,
    send_sems, recv_sems,
):
    me = lax.axis_index(AXES)
    entered = greet(me, devices)
    rows, width = zx_ref.shape
    total = recv_ref.shape[0]
    head_dim = width // HEADS
    block = 256
    lanes = 128
    per_group = 4
    gw = per_group * head_dim

    bits = (PATCH - 1).bit_length()
    seg = seg_ref[...] - seg_ref[:, 0:1]
    row = lax.broadcasted_iota(I32, (lanes, rows), 0)
    code = ((seg >> (row >> 1)) & 1) ^ (row & 1)
    fq_ref[...] = jnp.where((row < 2 * bits) & (code == 1), 1.0, 0.0).astype(BF)
    lane = lax.broadcasted_iota(I32, (rows, lanes), 1)
    seg_col = jnp.broadcast_to(seg, (lanes, rows)).T
    code = ((seg_col >> (lane >> 1)) & 1) ^ (lane & 1)
    fk = jnp.where((lane < 2 * bits) & (code == 0), -1e30, 0.0).astype(BF)
    for g in range(HEADS // per_group):
        kx_ref[g, :, 2 * gw : 2 * gw + lanes] = fk

    def unpack(i, carry):
        at = pl.ds(pl.multiple_of(i * block, block), block)
        z = dot(pick(slot_row_ref[...] - i * block, block, total, 0), recv_ref[...])
        zx_ref[at, :] = z.astype(BF)
        normed = layer_norm(z).astype(BF)
        normed_ref[at, :] = normed
        k = dot(normed, w_qkv_ref[:, width : 2 * width]).astype(BF)
        for g in range(HEADS // per_group):
            part = k[:, g * gw : (g + 1) * gw]
            kx_ref[g, at, 0 : 2 * gw] = jnp.concatenate([part, part], axis=1)
        return carry

    lax.fori_loop(0, rows // block, unpack, 0)
    normed = normed_ref[...]
    tn = (((0,), (1,)), ((), ()))
    q = lax.dot_general(w_qkv_ref[:, :width], normed, tn, preferred_element_type=F32)
    q = q.astype(BF).astype(F32) * (head_dim**-0.5 * math.log2(math.e))
    high = q.astype(BF)
    qh_ref[...] = high
    ql_ref[...] = (q - high.astype(F32)).astype(BF)
    v = lax.dot_general(w_qkv_ref[:, 2 * width :], normed, tn, preferred_element_type=F32)
    v_ref[...] = v.astype(BF)

    qb = 256
    units = rows // qb
    heads_a_step = 2
    ahead = 2
    slots = 4
    row_head = lax.broadcasted_iota(I32, (gw, qb), 0) // head_dim

    def weights(h, b):
        cols = slice(b * qb, (b + 1) * qb)
        at = pl.ds(pl.multiple_of((h // per_group) * gw, gw), gw)
        mine = row_head == h % per_group
        zero = jnp.zeros((), BF)
        return jnp.concatenate(
            [
                jnp.where(mine, qh_ref[at, cols], zero),
                jnp.where(mine, ql_ref[at, cols], zero),
                fq_ref[:, cols],
            ],
            axis=0,
        )

    def score(h, b, slot):
        s = dot(kx_ref[h // per_group], weights(h, b))
        s_ref[slot] = s
        m_ref[slot] = jnp.max(s.reshape(rows // 8, 8, qb), axis=0)

    for u in range(ahead):
        score(u // units, u % units, u % slots)

    def step(i, carry):
        for u in range(heads_a_step * units):
            h, b, cur = i * heads_a_step + u // units, u % units, u % slots
            nxt = u + ahead
            top = jnp.max(m_ref[cur], axis=0, keepdims=True)
            score(
                jnp.minimum(i * heads_a_step + nxt // units, HEADS - 1), nxt % units, nxt % slots
            )
            own = pl.ds(pl.multiple_of(h * head_dim, head_dim), head_dim)
            values = jnp.concatenate([v_ref[own, :], jnp.ones((head_dim, rows), BF)], axis=0)
            acc = None
            for c in range(rows // block):
                at = slice(c * block, (c + 1) * block)
                probs = jnp.exp2(s_ref[cur, at, :] - top).astype(BF)
                part = dot(values[:, at], probs)
                acc = part if acc is None else acc + part
            att = acc[:head_dim] / acc[head_dim : head_dim + 1]
            att_ref[own, b * qb : (b + 1) * qb] = att.astype(BF)
        return carry

    lax.fori_loop(0, HEADS // heads_a_step, step, 0)

    logit_ref[...] = jnp.zeros_like(logit_ref)
    for start in range(0, rows, block):
        at = slice(start, start + block)
        o = lax.dot_general(
            att_ref[:, at], w_out_ref[...], (((0,), (0,)), ((), ())), preferred_element_type=F32
        ).astype(BF)
        x_two = zx_ref[at, :].astype(F32) + o.astype(F32)
        hidden = gelu(dot(layer_norm(x_two).astype(BF), w_up_ref[...])).astype(BF)
        x_three = x_two + dot(hidden, w_down_ref[...])
        logit_ref[0:classes, at] = dot_nt(w_cls_ref[...], layer_norm(x_three).astype(BF))

    logits = logit_ref[...]
    high = logits.astype(BF)
    low = (logits - high.astype(F32)).astype(BF)
    both = jnp.concatenate([high, low], axis=0)
    half = high.shape[0]
    step_lanes = min(512, total)
    entered()
    for start in range(0, total, step_lanes):
        got = dot(both, pick(slot_row_ref[:, start : start + step_lanes], rows, step_lanes, 0))
        got = got.astype(BF)
        for d in range(step_lanes // capacity):
            at = slice(d * capacity, (d + 1) * capacity)
            back_ref[start // capacity + d] = jnp.concatenate([got[:half, at], got[half:, at]], axis=1)
    spread(back_ref, ret_ref, send_sems, recv_sems, me, devices)
    ret_ref[me] = back_ref[me]
    gather_in(back_ref, ret_ref, send_sems, recv_sems, me, devices)
    for d in range(devices):
        at = slice(d * capacity, (d + 1) * capacity)
        home_ref[0:half, at] = ret_ref[d, :, 0:capacity]
        home_ref[half : 2 * half, at] = ret_ref[d, :, capacity : 2 * capacity]
    returned = home_ref[...]
    for start in range(0, rows, block):
        at = slice(start, start + block)
        home = dot(returned, pick(pos_ref[:, at], total, block, 0))
        out_ref[:, at] = home[0:classes] + home[half : half + classes]


def local(
    coarse_feats,
    fine_feats,
    parent_index,
    nbr_offset,
    z_position,
    segment_id,
    w_parent,
    w_skip,
    conv_taps,
    w_cpe,
    w_qkv,
    w_out,
    w_up,
    w_down,
    w_cls,
):
    fine_rows, width = fine_feats.shape
    coarse_rows = coarse_feats.shape[0]
    devices = lax.axis_size(AXES)
    capacity = 2 * fine_rows // devices
    total = devices * capacity
    assert fine_rows == PATCH

    fine_per_coarse = fine_rows // coarse_rows
    margin = coarse_rows // 2 + REACH // fine_per_coarse
    lanes = 128
    pair = pltpu.SemaphoreType.DMA((devices,))
    pos, slots, recv = pl.pallas_call(
        functools.partial(encode_kernel, devices, capacity, margin),
        out_shape=(
            jax.ShapeDtypeStruct((1, fine_rows), I32),
            jax.ShapeDtypeStruct((1, total), I32),
            jax.ShapeDtypeStruct((devices, capacity, width), BF),
        ),
        in_specs=[VM] * 9,
        out_specs=(VM,) * 3,
        scratch_shapes=[
            pltpu.VMEM((fine_rows, width), BF),
            pltpu.VMEM((devices, 1, capacity), I32),
            pltpu.VMEM((devices, 1, capacity), I32),
            pltpu.VMEM((coarse_rows + 2 * margin, width), BF),
            pltpu.VMEM((2, REACH, width), BF),
            pltpu.VMEM((2, 1, REACH), I32),
            pltpu.VMEM((fine_rows, width), F32),
            pltpu.VMEM((fine_rows + 2 * REACH, width), BF),
            pltpu.VMEM((devices, capacity, width), BF),
            pair, pair, pair, pair,
            pltpu.SemaphoreType.DMA((6,)),
            pltpu.SemaphoreType.DMA((6,)),
        ],
        compiler_params=pltpu.CompilerParams(collective_id=0, has_side_effects=True),
    )(
        z_position.reshape(1, fine_rows), coarse_feats, fine_feats,
        parent_index.reshape(1, fine_rows), nbr_offset,
        w_parent, w_skip, conv_taps, w_cpe,
    )
    classes = w_cls.shape[0]
    half = -(-classes // 16) * 16
    return pl.pallas_call(
        functools.partial(decode_kernel, devices, capacity, classes),
        out_shape=jax.ShapeDtypeStruct((classes, fine_rows), F32),
        in_specs=[VM] * 9,
        out_specs=VM,
        scratch_shapes=[
            pltpu.VMEM((fine_rows, width), BF),
            pltpu.VMEM((fine_rows, width), BF),
            pltpu.VMEM((HEADS // 4, fine_rows, width // 2 + lanes), BF),
            pltpu.VMEM((width, fine_rows), BF),
            pltpu.VMEM((width, fine_rows), BF),
            pltpu.VMEM((width, fine_rows), BF),
            pltpu.VMEM((lanes, fine_rows), BF),
            pltpu.VMEM((4, fine_rows, 256), F32),
            pltpu.VMEM((4, 8, 256), F32),
            pltpu.VMEM((width, fine_rows), BF),
            pltpu.VMEM((half, fine_rows), F32),
            pltpu.VMEM((devices, half, 2 * capacity), BF),
            pltpu.VMEM((devices, half, 2 * capacity), BF),
            pltpu.VMEM((2 * half, total), BF),
            pair, pair,
        ],
        compiler_params=pltpu.CompilerParams(
            collective_id=1, has_side_effects=True, vmem_limit_bytes=48 * 2**20
        ),
    )(
        recv.reshape(total, width), slots, segment_id.reshape(1, fine_rows), pos,
        w_qkv, w_out, w_up, w_down, w_cls,
    )


def solution(mesh):
    rows = P(AXES, None)
    flat = P(AXES)
    placed = (rows, rows, flat, P(None, AXES), flat, flat) + (P(),) * 9
    return jax.shard_map(
        local, mesh=mesh, in_specs=placed, out_specs=P(None, AXES), check_vma=False
    )
```

```python
import functools
import math

import jax
import jax.numpy as jnp
from jax import lax
from jax.experimental import pallas as pl
from jax.experimental.pallas import tpu as pltpu
from jax.sharding import PartitionSpec as P

HEADS = 16
PATCH = 1024
REACH = 256
AXES = ("row", "col")
BF = jnp.bfloat16
F32 = jnp.float32
I32 = jnp.int32
VM = pl.BlockSpec(memory_space=pltpu.VMEM)


def dot(a, b):
    return jnp.dot(a, b, preferred_element_type=F32)


def dot_nt(a, b):
    return lax.dot_general(a, b, (((1,), (1,)), ((), ())), preferred_element_type=F32)


def layer_norm(values):
    center = values - jnp.mean(values, axis=-1, keepdims=True)
    spread = jnp.mean(center * center, axis=-1, keepdims=True)
    return center * lax.rsqrt(spread + 1e-05)


def pick(index, rows, cols, dim):
    grid = lax.broadcasted_iota(I32, (rows, cols), dim)
    return jnp.where(grid == index, 1.0, 0.0).astype(BF)


def column(row):
    return jnp.broadcast_to(row, (128, row.shape[1])).T[:, :1]


def place(device):
    inner = lax.axis_size("col")
    return (device // inner, device % inner)


def greet(me, devices):
    barrier = pltpu.get_barrier_semaphore()

    def signal(k, carry):
        pl.semaphore_signal(
            barrier, inc=1, device_id=place((me + k) % devices),
            device_id_type=pl.DeviceIdType.MESH,
        )
        return carry

    lax.fori_loop(1, devices, signal, 0)
    return lambda: pl.semaphore_wait(barrier, devices - 1)


def ship(src, dst, send_sem, recv_sem, device):
    return pltpu.make_async_remote_copy(
        src_ref=src, dst_ref=dst, send_sem=send_sem, recv_sem=recv_sem,
        device_id=place(device), device_id_type=pl.DeviceIdType.MESH,
    )


def spread(src_ref, dst_ref, send_sems, recv_sems, me, devices):
    def start(k, carry):
        peer = (me + k) % devices
        ship(
            src_ref.at[peer], dst_ref.at[me], send_sems.at[peer], recv_sems.at[me], peer
        ).start()
        return carry

    lax.fori_loop(1, devices, start, 0)


def gather_in(src_ref, dst_ref, send_sems, recv_sems, me, devices):
    def finish(k, carry):
        peer = (me + k) % devices
        ship(
            src_ref.at[peer], dst_ref.at[peer], send_sems.at[peer], recv_sems.at[peer], peer
        ).wait()
        return carry

    lax.fori_loop(1, devices, finish, 0)


def gelu(x):
    half = 0.5 * x
    return half + half * jnp.tanh(x * (0.7978845608028654 + 0.035677408136300125 * (x * x)))


def kernel(
    devices, capacity, margin, classes,
    z_ref, coarse_ref, fine_ref, parent_ref, nbr_ref, seg_ref,
    w_parent_ref, w_skip_ref, taps_ref, w_cpe_ref,
    w_qkv_ref, w_out_ref, w_up_ref, w_down_ref, w_cls_ref,
    out_ref,
    pos_ref, got_ref, share_ref, slot_ref, take_ref, par_ref, skip_ref, feat_ref, x_ref, send_ref, recv_ref,
    z_sum_ref, zx_ref, normed_ref, kx_ref, qh_ref, ql_ref, v_ref, fq_ref, s_ref, m_ref, att_ref,
    logit_ref, back_ref, ret_ref, home_ref,
    slot_send, slot_recv, feat_send, feat_recv, back_send, back_recv, side_send, side_recv,
):
    me = lax.axis_index(AXES)
    entered = greet(me, devices)
    rows, width = fine_ref.shape
    coarse_rows = coarse_ref.shape[0]
    coarse = par_ref.shape[0]
    total = devices * capacity
    head_dim = width // HEADS
    block = 256
    lanes = 128
    per_group = 4
    gw = per_group * head_dim
    after, before = (me + 1) % devices, (me + devices - 1) % devices

    par_ref[margin : margin + coarse_rows, :] = jax.nn.gelu(
        layer_norm(dot(coarse_ref[...], w_parent_ref[...]))
    ).astype(BF)
    entered()
    margins = [
        ship(
            par_ref.at[pl.ds(coarse_rows, margin), :], par_ref.at[pl.ds(0, margin), :],
            side_send.at[0], side_recv.at[0], after,
        ),
        ship(
            par_ref.at[pl.ds(margin, margin), :],
            par_ref.at[pl.ds(margin + coarse_rows, margin), :],
            side_send.at[1], side_recv.at[1], before,
        ),
    ]
    for move in margins:
        move.start()

    def skips(i, carry):
        at = pl.ds(pl.multiple_of(i * block, block), block)
        skip_ref[at, :] = jax.nn.gelu(layer_norm(dot(fine_ref[at, :], w_skip_ref[...])))
        return carry

    lax.fori_loop(0, rows // block, skips, 0)

    z = z_ref[...]
    dest = z // rows
    slot = z % rows
    onehot = pick(dest, devices, rows, 0)
    earlier = lax.broadcasted_iota(I32, (rows, rows), 0) < lax.broadcasted_iota(I32, (rows, rows), 1)
    ahead_of = dot(onehot, jnp.where(earlier, 1.0, 0.0).astype(BF))
    rank = jnp.sum(ahead_of * onehot.astype(F32), axis=0, keepdims=True).astype(I32)
    pos = dest * capacity + rank
    pos_ref[...] = pos

    base_row = me * coarse_rows - margin
    for move in margins:
        move.wait()

    def join(i):
        base = i * block
        at = slice(base, base + block)
        chosen = dot(pick(column(parent_ref[:, at] - base_row), block, coarse, 1), par_ref[...])
        feat_ref[base + REACH : base + REACH + block, :] = (chosen + skip_ref[at, :]).astype(BF)

    blocks = rows // block
    edges = [
        ship(
            feat_ref.at[pl.ds(rows, REACH), :], feat_ref.at[pl.ds(0, REACH), :],
            side_send.at[2], side_recv.at[2], after,
        ),
        ship(
            feat_ref.at[pl.ds(REACH, REACH), :], feat_ref.at[pl.ds(REACH + rows, REACH), :],
            side_send.at[3], side_recv.at[3], before,
        ),
    ]
    join(blocks - 1)
    edges[0].start()
    join(0)
    edges[1].start()
    for i in range(1, blocks - 1):
        join(i)

    code = slot + 1
    part = lax.broadcasted_iota(I32, (16, rows), 0)
    digits = jnp.where(part == 0, code // 32, jnp.where(part == 1, code % 32, 0))
    digits = digits.astype(F32).astype(BF)
    piece = min(512, total)
    for start in range(0, total, piece):
        got = dot_nt(digits, pick(pos - start, piece, rows, 0)).astype(I32)
        got = got[0:1] * 32 + got[1:2] - 1
        for d in range(piece // capacity):
            slot_ref[start // capacity + d] = got[:, d * capacity : (d + 1) * capacity]
    spread(slot_ref, take_ref, slot_send, slot_recv, me, devices)
    take_ref[me] = slot_ref[me]

    window = block + 2 * REACH

    def conv(i, carry):
        base = pl.multiple_of(i * block, block)
        at = pl.ds(base, block)
        cells = feat_ref[pl.ds(base, window), :]
        offsets = nbr_ref[:, at].T
        here = lax.broadcasted_iota(I32, offsets.shape, 0) + REACH
        source = jnp.where(offsets != REACH + 1, here + offsets, -1)
        acc = jnp.zeros((block, cells.shape[1]), F32)
        for t in range(nbr_ref.shape[0]):
            acc = acc + dot(pick(source[:, t : t + 1], block, window, 1), cells) * taps_ref[t : t + 1, :]
        out = layer_norm(dot(acc.astype(BF), w_cpe_ref[...]))
        center = feat_ref[pl.ds(base + REACH, block), :]
        x_ref[at, :] = (center.astype(F32) + out).astype(BF)
        return carry

    lax.fori_loop(1, blocks - 1, conv, 0)
    for move in edges:
        move.wait()
    lax.fori_loop(0, 2, lambda i, carry: conv(i * (blocks - 1), carry), 0)

    pos = pos_ref[...]
    per = block // capacity
    shares = devices // per
    stride = 2

    def block_of(j):
        half = shares // stride
        shift = jnp.where(j < half, stride * j + 1, stride * (j - half) + 2)
        return (me // per + shift) % shares

    def pack(j, carry):
        b = block_of(j)
        sent = dot(pick(pos - b * block, block, rows, 0), x_ref[...]).astype(BF)
        send_ref[pl.ds(b * per, per)] = sent.reshape(per, capacity, width)

        def start(k, inner):
            peer = b * per + k

            @pl.when(peer != me)
            def _():
                ship(
                    send_ref.at[peer], recv_ref.at[me], feat_send.at[peer], feat_recv.at[me], peer
                ).start()

            return inner

        lax.fori_loop(0, per, start, 0)
        return carry

    lax.fori_loop(0, shares, pack, 0)
    recv_ref[me] = send_ref[me]

    bits = (PATCH - 1).bit_length()
    seg = seg_ref[...] - seg_ref[:, 0:1]
    row = lax.broadcasted_iota(I32, (lanes, rows), 0)
    code = ((seg >> (row >> 1)) & 1) ^ (row & 1)
    fq_ref[...] = jnp.where((row < 2 * bits) & (code == 1), 1.0, 0.0).astype(BF)
    lane = lax.broadcasted_iota(I32, (rows, lanes), 1)
    seg_col = jnp.broadcast_to(seg, (lanes, rows)).T
    code = ((seg_col >> (lane >> 1)) & 1) ^ (lane & 1)
    fk = jnp.where((lane < 2 * bits) & (code == 0), -1e30, 0.0).astype(BF)
    for g in range(HEADS // per_group):
        kx_ref[g, :, 2 * gw : 2 * gw + lanes] = fk


    gather_in(slot_ref, take_ref, slot_send, slot_recv, me, devices)
    for d in range(devices):
        got_ref[:, d * capacity : (d + 1) * capacity] = take_ref[d]
    z_sum_ref[...] = jnp.zeros_like(z_sum_ref)
    for d in range(shares):
        share_ref[d] = got_ref[:, d * block : (d + 1) * block]

    def collect(j, carry):
        b = block_of(shares - 1 - j)

        def finish(k, inner):
            peer = b * per + k

            @pl.when(peer != me)
            def _():
                ship(
                    send_ref.at[peer], recv_ref.at[peer], feat_send.at[peer], feat_recv.at[peer], peer
                ).wait()

            return inner

        lax.fori_loop(0, per, finish, 0)
        came = recv_ref[pl.ds(b * per, per)].reshape(block, width)
        z_sum_ref[...] += dot(pick(share_ref[b], rows, block, 0), came)
        return carry

    lax.fori_loop(0, shares, collect, 0)

    def project(i, carry):
        at = pl.ds(pl.multiple_of(i * block, block), block)
        z = z_sum_ref[at, :]
        zx_ref[at, :] = z.astype(BF)
        normed = layer_norm(z).astype(BF)
        normed_ref[at, :] = normed
        k = dot(normed, w_qkv_ref[:, width : 2 * width]).astype(BF)
        for g in range(HEADS // per_group):
            part = k[:, g * gw : (g + 1) * gw]
            kx_ref[g, at, 0 : 2 * gw] = jnp.concatenate([part, part], axis=1)
        return carry

    lax.fori_loop(0, blocks, project, 0)
    normed = normed_ref[...]
    tn = (((0,), (1,)), ((), ()))
    q = lax.dot_general(w_qkv_ref[:, :width], normed, tn, preferred_element_type=F32)
    q = q.astype(BF).astype(F32) * (head_dim**-0.5 * math.log2(math.e))
    high = q.astype(BF)
    qh_ref[...] = high
    ql_ref[...] = (q - high.astype(F32)).astype(BF)
    v = lax.dot_general(w_qkv_ref[:, 2 * width :], normed, tn, preferred_element_type=F32)
    v_ref[...] = v.astype(BF)

    qb = 256
    units = rows // qb
    heads_a_step = 2
    ahead = 2
    slots = 4
    row_head = lax.broadcasted_iota(I32, (gw, qb), 0) // head_dim

    def weights(h, b):
        cols = slice(b * qb, (b + 1) * qb)
        at = pl.ds(pl.multiple_of((h // per_group) * gw, gw), gw)
        mine = row_head == h % per_group
        zero = jnp.zeros((), BF)
        return jnp.concatenate(
            [
                jnp.where(mine, qh_ref[at, cols], zero),
                jnp.where(mine, ql_ref[at, cols], zero),
                fq_ref[:, cols],
            ],
            axis=0,
        )

    def score(h, b, slot):
        s = dot(kx_ref[h // per_group], weights(h, b))
        s_ref[slot] = s
        m_ref[slot] = jnp.max(s.reshape(rows // 8, 8, qb), axis=0)

    for u in range(ahead):
        score(u // units, u % units, u % slots)

    def step(i, carry):
        for u in range(heads_a_step * units):
            h, b, cur = i * heads_a_step + u // units, u % units, u % slots
            nxt = u + ahead
            top = jnp.max(m_ref[cur], axis=0, keepdims=True)
            score(
                jnp.minimum(i * heads_a_step + nxt // units, HEADS - 1), nxt % units, nxt % slots
            )
            own = pl.ds(pl.multiple_of(h * head_dim, head_dim), head_dim)
            values = jnp.concatenate([v_ref[own, :], jnp.ones((head_dim, rows), BF)], axis=0)
            acc = None
            for c in range(rows // block):
                at = slice(c * block, (c + 1) * block)
                probs = jnp.exp2(s_ref[cur, at, :] - top).astype(BF)
                part = dot(values[:, at], probs)
                acc = part if acc is None else acc + part
            att = acc[:head_dim] / acc[head_dim : head_dim + 1]
            att_ref[own, b * qb : (b + 1) * qb] = att.astype(BF)
        return carry

    lax.fori_loop(0, HEADS // heads_a_step, step, 0)

    logit_ref[...] = jnp.zeros_like(logit_ref)
    for start in range(0, rows, block):
        at = slice(start, start + block)
        o = lax.dot_general(
            att_ref[:, at], w_out_ref[...], (((0,), (0,)), ((), ())), preferred_element_type=F32
        ).astype(BF)
        x_two = zx_ref[at, :].astype(F32) + o.astype(F32)
        hidden = gelu(dot(layer_norm(x_two).astype(BF), w_up_ref[...])).astype(BF)
        x_three = x_two + dot(hidden, w_down_ref[...])
        logit_ref[0:classes, at] = dot_nt(w_cls_ref[...], layer_norm(x_three).astype(BF))

    logits = logit_ref[...]
    high = logits.astype(BF)
    low = (logits - high.astype(F32)).astype(BF)
    both = jnp.concatenate([high, low], axis=0)
    half = high.shape[0]
    step_lanes = min(512, total)
    for start in range(0, total, step_lanes):
        got = dot(both, pick(got_ref[:, start : start + step_lanes], rows, step_lanes, 0))
        got = got.astype(BF)
        for d in range(step_lanes // capacity):
            at = slice(d * capacity, (d + 1) * capacity)
            back_ref[start // capacity + d] = jnp.concatenate([got[:half, at], got[half:, at]], axis=1)
    spread(back_ref, ret_ref, back_send, back_recv, me, devices)
    ret_ref[me] = back_ref[me]
    gather_in(back_ref, ret_ref, back_send, back_recv, me, devices)
    for d in range(devices):
        at = slice(d * capacity, (d + 1) * capacity)
        home_ref[0:half, at] = ret_ref[d, :, 0:capacity]
        home_ref[half : 2 * half, at] = ret_ref[d, :, capacity : 2 * capacity]
    returned = home_ref[...]
    for start in range(0, rows, block):
        at = slice(start, start + block)
        home = dot(returned, pick(pos_ref[:, at], total, block, 0))
        out_ref[:, at] = home[0:classes] + home[half : half + classes]


def local(
    coarse_feats,
    fine_feats,
    parent_index,
    nbr_offset,
    z_position,
    segment_id,
    w_parent,
    w_skip,
    conv_taps,
    w_cpe,
    w_qkv,
    w_out,
    w_up,
    w_down,
    w_cls,
):
    fine_rows, width = fine_feats.shape
    coarse_rows = coarse_feats.shape[0]
    devices = lax.axis_size(AXES)
    capacity = 2 * fine_rows // devices
    total = devices * capacity
    assert fine_rows == PATCH

    margin = coarse_rows // 2
    lanes = 128
    classes = w_cls.shape[0]
    half = -(-classes // 16) * 16
    pair = pltpu.SemaphoreType.DMA((devices,))
    side = pltpu.SemaphoreType.DMA((4,))
    return pl.pallas_call(
        functools.partial(kernel, devices, capacity, margin, classes),
        out_shape=jax.ShapeDtypeStruct((classes, fine_rows), F32),
        in_specs=[VM] * 15,
        out_specs=VM,
        scratch_shapes=[
            pltpu.VMEM((1, fine_rows), I32),
            pltpu.VMEM((1, total), I32),
            pltpu.VMEM((total // 256, 1, 256), I32),
            pltpu.VMEM((devices, 1, capacity), I32),
            pltpu.VMEM((devices, 1, capacity), I32),
            pltpu.VMEM((coarse_rows + 2 * margin, width), BF),
            pltpu.VMEM((fine_rows, width), F32),
            pltpu.VMEM((fine_rows + 2 * REACH, width), BF),
            pltpu.VMEM((fine_rows, width), BF),
            pltpu.VMEM((devices, capacity, width), BF),
            pltpu.VMEM((devices, capacity, width), BF),
            pltpu.VMEM((fine_rows, width), F32),
            pltpu.VMEM((fine_rows, width), BF),
            pltpu.VMEM((fine_rows, width), BF),
            pltpu.VMEM((HEADS // 4, fine_rows, width // 2 + lanes), BF),
            pltpu.VMEM((width, fine_rows), BF),
            pltpu.VMEM((width, fine_rows), BF),
            pltpu.VMEM((width, fine_rows), BF),
            pltpu.VMEM((lanes, fine_rows), BF),
            pltpu.VMEM((4, fine_rows, 256), F32),
            pltpu.VMEM((4, 8, 256), F32),
            pltpu.VMEM((width, fine_rows), BF),
            pltpu.VMEM((half, fine_rows), F32),
            pltpu.VMEM((devices, half, 2 * capacity), BF),
            pltpu.VMEM((devices, half, 2 * capacity), BF),
            pltpu.VMEM((2 * half, total), BF),
            pair, pair, pair, pair, pair, pair, side, side,
        ],
        compiler_params=pltpu.CompilerParams(
            collective_id=0, has_side_effects=True, vmem_limit_bytes=60 * 2**20
        ),
    )(
        z_position.reshape(1, fine_rows), coarse_feats, fine_feats,
        parent_index.reshape(1, fine_rows), nbr_offset, segment_id.reshape(1, fine_rows),
        w_parent, w_skip, conv_taps, w_cpe, w_qkv, w_out, w_up, w_down, w_cls,
    )


def solution(mesh):
    rows = P(AXES, None)
    flat = P(AXES)
    placed = (rows, rows, flat, P(None, AXES), flat, flat) + (P(),) * 9
    return jax.shard_map(
        local, mesh=mesh, in_specs=placed, out_specs=P(None, AXES), check_vma=False
    )
```

```python
import functools
import math

import jax
import jax.numpy as jnp
from jax import lax
from jax.experimental import pallas as pl
from jax.experimental.pallas import tpu as pltpu
from jax.sharding import PartitionSpec as P

HEADS = 16
PATCH = 1024
REACH = 256
AXES = ("row", "col")
BF = jnp.bfloat16
F32 = jnp.float32
I32 = jnp.int32
I16 = jnp.int16
VM = pl.BlockSpec(memory_space=pltpu.VMEM)


def dot(a, b):
    return jnp.dot(a, b, preferred_element_type=F32)


def dot_nt(a, b):
    return lax.dot_general(a, b, (((1,), (1,)), ((), ())), preferred_element_type=F32)


def layer_norm(values):
    center = values - jnp.mean(values, axis=-1, keepdims=True)
    spread = jnp.mean(center * center, axis=-1, keepdims=True)
    return center * lax.rsqrt(spread + 1e-05)


def gelu(x):
    half = 0.5 * x
    return half + half * jnp.tanh(x * (0.7978845608028654 + 0.035677408136300125 * (x * x)))


def pick(index, rows, cols, dim):
    grid = lax.broadcasted_iota(I16, (rows, cols), dim)
    if dim == 0:
        index = jnp.broadcast_to(index, (16, cols)).astype(I16)[0:1]
    else:
        index = jnp.broadcast_to(index, (rows, 128)).astype(I16)
        index = jnp.concatenate([index] * (cols // 128), axis=1)
    return jnp.where(grid == index, jnp.ones((), BF), jnp.zeros((), BF))


def column(row):
    return jnp.broadcast_to(row, (128, row.shape[1])).T[:, :1]


def place(device):
    inner = lax.axis_size("col")
    return (device // inner, device % inner)


def greet(me, devices):
    barrier = pltpu.get_barrier_semaphore()

    def signal(k, carry):
        pl.semaphore_signal(
            barrier, inc=1, device_id=place((me + k) % devices),
            device_id_type=pl.DeviceIdType.MESH,
        )
        return carry

    lax.fori_loop(1, devices, signal, 0)
    return lambda: pl.semaphore_wait(barrier, devices - 1)


def ship(src, dst, send_sem, recv_sem, device):
    return pltpu.make_async_remote_copy(
        src_ref=src, dst_ref=dst, send_sem=send_sem, recv_sem=recv_sem,
        device_id=place(device), device_id_type=pl.DeviceIdType.MESH,
    )


def spread(src_ref, dst_ref, send_sems, recv_sems, me, devices):
    def start(k, carry):
        peer = (me + k) % devices
        ship(
            src_ref.at[peer], dst_ref.at[me], send_sems.at[peer], recv_sems.at[me], peer
        ).start()
        return carry

    lax.fori_loop(1, devices, start, 0)


def gather_in(src_ref, dst_ref, send_sems, recv_sems, me, devices):
    def finish(k, carry):
        peer = (me + k) % devices
        ship(
            src_ref.at[peer], dst_ref.at[peer], send_sems.at[peer], recv_sems.at[peer], peer
        ).wait()
        return carry

    lax.fori_loop(1, devices, finish, 0)


def kernel(
    devices, capacity, margin, classes,
    z_ref, coarse_ref, fine_ref, parent_ref, nbr_ref, seg_ref,
    w_parent_ref, w_skip_ref, taps_ref, w_cpe_ref,
    w_qkv_hbm, w_out_hbm, w_up_hbm, w_down_hbm, w_cls_ref,
    out_ref,
    w_qkv_ref, w_out_ref, w_up_ref, w_down_ref,
    pos_ref, got_ref, share_ref, slot_ref, take_ref, par_ref, skip_ref, feat_ref, x_ref, send_ref, recv_ref,
    z_sum_ref, zx_ref, normed_ref, kx_ref, qh_ref, ql_ref, v_ref, fq_ref, s_ref, m_ref, att_ref,
    logit_ref, back_ref, ret_ref, part_ref, home_ref,
    slot_send, slot_recv, feat_send, feat_recv, back_send, back_recv, side_send, side_recv, load_sem,
):
    me = lax.axis_index(AXES)
    entered = greet(me, devices)
    loads = [
        pltpu.make_async_copy(src, dst, load_sem.at[i])
        for i, (src, dst) in enumerate(
            (
                (w_qkv_hbm, w_qkv_ref), (w_out_hbm, w_out_ref),
                (w_up_hbm, w_up_ref), (w_down_hbm, w_down_ref),
            )
        )
    ]
    for load in loads:
        load.start()
    rows, width = fine_ref.shape
    coarse_rows = coarse_ref.shape[0]
    coarse = par_ref.shape[0]
    total = devices * capacity
    head_dim = width // HEADS
    block = 256
    lanes = 128
    per_group = 4
    gw = per_group * head_dim
    after, before = (me + 1) % devices, (me + devices - 1) % devices

    par_ref[margin : margin + coarse_rows, :] = gelu(
        layer_norm(dot(coarse_ref[...], w_parent_ref[...]))
    ).astype(BF)
    entered()
    margins = [
        ship(
            par_ref.at[pl.ds(coarse_rows, margin), :], par_ref.at[pl.ds(0, margin), :],
            side_send.at[0], side_recv.at[0], after,
        ),
        ship(
            par_ref.at[pl.ds(margin, margin), :],
            par_ref.at[pl.ds(margin + coarse_rows, margin), :],
            side_send.at[1], side_recv.at[1], before,
        ),
    ]
    for move in margins:
        move.start()

    def skips(i, carry):
        at = pl.ds(pl.multiple_of(i * block, block), block)
        skip_ref[at, :] = gelu(layer_norm(dot(fine_ref[at, :], w_skip_ref[...])))
        return carry

    lax.fori_loop(0, rows // block, skips, 0)

    z = z_ref[...]
    dest = z // rows
    slot = z % rows
    onehot = pick(dest, devices, rows, 0)
    earlier = lax.broadcasted_iota(I32, (rows, rows), 0) < lax.broadcasted_iota(I32, (rows, rows), 1)
    ahead_of = dot(onehot, jnp.where(earlier, 1.0, 0.0).astype(BF))
    rank = jnp.sum(ahead_of * onehot.astype(F32), axis=0, keepdims=True).astype(I32)
    pos = dest * capacity + rank
    pos_ref[...] = pos

    code = slot + 1
    part = lax.broadcasted_iota(I32, (16, rows), 0)
    digits = jnp.where(part == 0, code // 32, jnp.where(part == 1, code % 32, 0))
    digits = digits.astype(F32).astype(BF)
    piece = min(512, total)
    for start in range(0, total, piece):
        got = dot_nt(digits, pick(pos - start, piece, rows, 0)).astype(I32)
        got = got[0:1] * 32 + got[1:2] - 1
        for d in range(piece // capacity):
            slot_ref[start // capacity + d] = got[:, d * capacity : (d + 1) * capacity]
    spread(slot_ref, take_ref, slot_send, slot_recv, me, devices)
    take_ref[me] = slot_ref[me]

    base_row = me * coarse_rows - margin
    for move in margins:
        move.wait()

    def join(i):
        base = i * block
        at = slice(base, base + block)
        chosen = dot(pick(column(parent_ref[:, at] - base_row), block, coarse, 1), par_ref[...])
        feat_ref[base + REACH : base + REACH + block, :] = (chosen + skip_ref[at, :]).astype(BF)

    blocks = rows // block
    edges = [
        ship(
            feat_ref.at[pl.ds(rows, REACH), :], feat_ref.at[pl.ds(0, REACH), :],
            side_send.at[2], side_recv.at[2], after,
        ),
        ship(
            feat_ref.at[pl.ds(REACH, REACH), :], feat_ref.at[pl.ds(REACH + rows, REACH), :],
            side_send.at[3], side_recv.at[3], before,
        ),
    ]
    join(blocks - 1)
    edges[0].start()
    join(0)
    edges[1].start()
    for i in range(1, blocks - 1):
        join(i)

    window = block + 2 * REACH

    def conv(i, carry):
        base = pl.multiple_of(i * block, block)
        at = pl.ds(base, block)
        cells = feat_ref[pl.ds(base, window), :]
        offsets = nbr_ref[:, at].T
        here = lax.broadcasted_iota(I32, offsets.shape, 0) + REACH
        source = jnp.where(offsets != REACH + 1, here + offsets, -1)
        acc = jnp.zeros((block, cells.shape[1]), F32)
        for t in range(nbr_ref.shape[0]):
            acc = acc + dot(pick(source[:, t : t + 1], block, window, 1), cells) * taps_ref[t : t + 1, :]
        out = layer_norm(dot(acc.astype(BF), w_cpe_ref[...]))
        center = feat_ref[pl.ds(base + REACH, block), :]
        x_ref[at, :] = (center.astype(F32) + out).astype(BF)
        return carry

    lax.fori_loop(1, blocks - 1, conv, 0)
    for move in edges:
        move.wait()
    lax.fori_loop(0, 2, lambda i, carry: conv(i * (blocks - 1), carry), 0)

    pos = pos_ref[...]
    per = block // capacity
    shares = devices // per
    stride = 2

    def block_of(j):
        half = shares // stride
        shift = jnp.where(j < half, stride * j + 1, stride * (j - half) + 2)
        return (me // per + shift) % shares

    def pack(j, carry):
        b = block_of(j)
        sent = dot(pick(pos - b * block, block, rows, 0), x_ref[...]).astype(BF)
        send_ref[pl.ds(b * per, per)] = sent.reshape(per, capacity, width)

        def start(k, inner):
            peer = b * per + k

            @pl.when(peer != me)
            def _():
                ship(
                    send_ref.at[peer], recv_ref.at[me], feat_send.at[peer], feat_recv.at[me], peer
                ).start()

            return inner

        lax.fori_loop(0, per, start, 0)
        return carry

    lax.fori_loop(0, shares, pack, 0)
    recv_ref[me] = send_ref[me]

    bits = (PATCH - 1).bit_length()
    seg = seg_ref[...] - seg_ref[:, 0:1]
    row = lax.broadcasted_iota(I32, (lanes, rows), 0)
    code = ((seg >> (row >> 1)) & 1) ^ (row & 1)
    fq_ref[...] = jnp.where((row < 2 * bits) & (code == 1), 1.0, 0.0).astype(BF)
    lane = lax.broadcasted_iota(I32, (rows, lanes), 1)
    seg_col = jnp.broadcast_to(seg, (lanes, rows)).T
    code = ((seg_col >> (lane >> 1)) & 1) ^ (lane & 1)
    fk = jnp.where((lane < 2 * bits) & (code == 0), -1e30, 0.0).astype(BF)
    for g in range(HEADS // per_group):
        kx_ref[g, :, 2 * gw : 2 * gw + lanes] = fk


    gather_in(slot_ref, take_ref, slot_send, slot_recv, me, devices)
    for d in range(devices):
        got_ref[:, d * capacity : (d + 1) * capacity] = take_ref[d]
    z_sum_ref[...] = jnp.zeros_like(z_sum_ref)
    for load in loads:
        load.wait()
    for d in range(shares):
        share_ref[d] = got_ref[:, d * block : (d + 1) * block]

    def collect(j, carry):
        b = block_of(shares - 1 - j)

        def finish(k, inner):
            peer = b * per + k

            @pl.when(peer != me)
            def _():
                ship(
                    send_ref.at[peer], recv_ref.at[peer], feat_send.at[peer], feat_recv.at[peer], peer
                ).wait()

            return inner

        lax.fori_loop(0, per, finish, 0)
        came = recv_ref[pl.ds(b * per, per)].reshape(block, width)
        z_sum_ref[...] += dot(pick(share_ref[b], rows, block, 0), came)
        return carry

    lax.fori_loop(0, shares, collect, 0)

    def project(i, carry):
        at = pl.ds(pl.multiple_of(i * block, block), block)
        z = z_sum_ref[at, :]
        zx_ref[at, :] = z.astype(BF)
        normed = layer_norm(z).astype(BF)
        normed_ref[at, :] = normed
        k = dot(normed, w_qkv_ref[:, width : 2 * width]).astype(BF)
        for g in range(HEADS // per_group):
            part = k[:, g * gw : (g + 1) * gw]
            kx_ref[g, at, 0 : 2 * gw] = jnp.concatenate([part, part], axis=1)
        return carry

    lax.fori_loop(0, blocks, project, 0)
    normed = normed_ref[...]
    tn = (((0,), (1,)), ((), ()))
    q = lax.dot_general(w_qkv_ref[:, :width], normed, tn, preferred_element_type=F32)
    q = q.astype(BF).astype(F32) * (head_dim**-0.5 * math.log2(math.e))
    high = q.astype(BF)
    qh_ref[...] = high
    ql_ref[...] = (q - high.astype(F32)).astype(BF)
    v = lax.dot_general(w_qkv_ref[:, 2 * width :], normed, tn, preferred_element_type=F32)
    v_ref[...] = v.astype(BF)

    qb = 256
    units = rows // qb
    heads_a_step = 4
    ahead = 2
    slots = 4
    row_head = lax.broadcasted_iota(I32, (gw, qb), 0) // head_dim

    def weights(h, b):
        cols = slice(b * qb, (b + 1) * qb)
        at = pl.ds(pl.multiple_of((h // per_group) * gw, gw), gw)
        mine = row_head == h % per_group
        zero = jnp.zeros((), BF)
        return jnp.concatenate(
            [
                jnp.where(mine, qh_ref[at, cols], zero),
                jnp.where(mine, ql_ref[at, cols], zero),
                fq_ref[:, cols],
            ],
            axis=0,
        )

    def score(h, b, slot):
        w = weights(h, b)
        top = None
        for start in range(0, rows, 512):
            s = dot(kx_ref[h // per_group, start : start + 512, :], w)
            s_ref[slot, start : start + 512, :] = s
            part = jnp.max(s.reshape(512 // 8, 8, qb), axis=0)
            top = part if top is None else jnp.maximum(top, part)
        m_ref[slot] = top

    for u in range(ahead):
        score(u // units, u % units, u % slots)

    def step(i, carry):
        for u in range(heads_a_step * units):
            h, b, cur = i * heads_a_step + u // units, u % units, u % slots
            nxt = u + ahead
            top = jnp.max(m_ref[cur], axis=0, keepdims=True)
            score(
                jnp.minimum(i * heads_a_step + nxt // units, HEADS - 1), nxt % units, nxt % slots
            )
            own = pl.ds(pl.multiple_of(h * head_dim, head_dim), head_dim)
            values = jnp.concatenate([v_ref[own, :], jnp.ones((head_dim, rows), BF)], axis=0)
            acc = None
            for c in range(rows // block):
                at = slice(c * block, (c + 1) * block)
                probs = jnp.exp2(s_ref[cur, at, :] - top).astype(BF)
                part = dot(values[:, at], probs)
                acc = part if acc is None else acc + part
            att = acc[:head_dim] / acc[head_dim : head_dim + 1]
            att_ref[own, b * qb : (b + 1) * qb] = att.astype(BF)
        return carry

    lax.fori_loop(0, HEADS // heads_a_step, step, 0)

    logit_ref[...] = jnp.zeros_like(logit_ref)
    for start in range(0, rows, block):
        at = slice(start, start + block)
        o = lax.dot_general(
            att_ref[:, at], w_out_ref[...], (((0,), (0,)), ((), ())), preferred_element_type=F32
        ).astype(BF)
        x_two = zx_ref[at, :].astype(F32) + o.astype(F32)
        hidden = gelu(dot(layer_norm(x_two).astype(BF), w_up_ref[...]).astype(BF))
        x_three = x_two + dot(hidden, w_down_ref[...])
        logit_ref[0:classes, at] = dot_nt(w_cls_ref[...], layer_norm(x_three).astype(BF))

    logits = logit_ref[...]
    high = logits.astype(BF)
    low = (logits - high.astype(F32)).astype(BF)
    both = jnp.concatenate([high, low], axis=0)
    half = high.shape[0]

    def give(j, carry):
        b = block_of(j)
        got = dot(both, pick(share_ref[b], rows, block, 0)).astype(BF)
        for d in range(per):
            at = slice(d * capacity, (d + 1) * capacity)
            back_ref[b * per + d] = jnp.concatenate([got[:half, at], got[half:, at]], axis=1)

        def start(k, inner):
            peer = b * per + k

            @pl.when(peer != me)
            def _():
                ship(
                    back_ref.at[peer], ret_ref.at[me], back_send.at[peer], back_recv.at[me], peer
                ).start()

            return inner

        lax.fori_loop(0, per, start, 0)
        return carry

    lax.fori_loop(0, shares, give, 0)
    ret_ref[me] = back_ref[me]
    home_ref[...] = jnp.zeros_like(home_ref)

    def take(j, carry):
        b = block_of(shares - 1 - j)

        def finish(k, inner):
            peer = b * per + k

            @pl.when(peer != me)
            def _():
                ship(
                    back_ref.at[peer], ret_ref.at[peer], back_send.at[peer], back_recv.at[peer], peer
                ).wait()

            return inner

        lax.fori_loop(0, per, finish, 0)
        for d in range(per):
            came = ret_ref[b * per + d]
            at = slice(d * capacity, (d + 1) * capacity)
            part_ref[0:half, at] = came[:, 0:capacity]
            part_ref[half : 2 * half, at] = came[:, capacity : 2 * capacity]
        home_ref[...] += dot(part_ref[...], pick(pos_ref[...] - b * block, block, rows, 0))
        return carry

    lax.fori_loop(0, shares, take, 0)
    out_ref[...] = home_ref[0:classes, :] + home_ref[half : half + classes, :]


def local(
    coarse_feats,
    fine_feats,
    parent_index,
    nbr_offset,
    z_position,
    segment_id,
    w_parent,
    w_skip,
    conv_taps,
    w_cpe,
    w_qkv,
    w_out,
    w_up,
    w_down,
    w_cls,
):
    fine_rows, width = fine_feats.shape
    coarse_rows = coarse_feats.shape[0]
    devices = lax.axis_size(AXES)
    capacity = 2 * fine_rows // devices
    total = devices * capacity
    assert fine_rows == PATCH

    margin = coarse_rows // 2
    lanes = 128
    classes = w_cls.shape[0]
    half = -(-classes // 16) * 16
    pair = pltpu.SemaphoreType.DMA((devices,))
    side = pltpu.SemaphoreType.DMA((4,))
    return pl.pallas_call(
        functools.partial(kernel, devices, capacity, margin, classes),
        out_shape=jax.ShapeDtypeStruct((classes, fine_rows), F32),
        in_specs=[VM] * 10 + [pl.BlockSpec(memory_space=pl.ANY)] * 4 + [VM],
        out_specs=VM,
        scratch_shapes=[
            *[pltpu.VMEM(w.shape, w.dtype) for w in (w_qkv, w_out, w_up, w_down)],
            pltpu.VMEM((1, fine_rows), I32),
            pltpu.VMEM((1, total), I32),
            pltpu.VMEM((total // 256, 1, 256), I32),
            pltpu.VMEM((devices, 1, capacity), I32),
            pltpu.VMEM((devices, 1, capacity), I32),
            pltpu.VMEM((coarse_rows + 2 * margin, width), BF),
            pltpu.VMEM((fine_rows, width), F32),
            pltpu.VMEM((fine_rows + 2 * REACH, width), BF),
            pltpu.VMEM((fine_rows, width), BF),
            pltpu.VMEM((devices, capacity, width), BF),
            pltpu.VMEM((devices, capacity, width), BF),
            pltpu.VMEM((fine_rows, width), F32),
            pltpu.VMEM((fine_rows, width), BF),
            pltpu.VMEM((fine_rows, width), BF),
            pltpu.VMEM((HEADS // 4, fine_rows, width // 2 + lanes), BF),
            pltpu.VMEM((width, fine_rows), BF),
            pltpu.VMEM((width, fine_rows), BF),
            pltpu.VMEM((width, fine_rows), BF),
            pltpu.VMEM((lanes, fine_rows), BF),
            pltpu.VMEM((4, fine_rows, 256), F32),
            pltpu.VMEM((4, 8, 256), F32),
            pltpu.VMEM((width, fine_rows), BF),
            pltpu.VMEM((half, fine_rows), F32),
            pltpu.VMEM((devices, half, 2 * capacity), BF),
            pltpu.VMEM((devices, half, 2 * capacity), BF),
            pltpu.VMEM((2 * half, 256), BF),
            pltpu.VMEM((2 * half, fine_rows), F32),
            pair, pair, pair, pair, pair, pair, side, side, side,
        ],
        compiler_params=pltpu.CompilerParams(
            collective_id=0, has_side_effects=True, vmem_limit_bytes=60 * 2**20
        ),
    )(
        z_position.reshape(1, fine_rows), coarse_feats, fine_feats,
        parent_index.reshape(1, fine_rows), nbr_offset, segment_id.reshape(1, fine_rows),
        w_parent, w_skip, conv_taps, w_cpe, w_qkv, w_out, w_up, w_down, w_cls,
    )


def solution(mesh):
    rows = P(AXES, None)
    flat = P(AXES)
    placed = (rows, rows, flat, P(None, AXES), flat, flat) + (P(),) * 9
    return jax.shard_map(
        local, mesh=mesh, in_specs=placed, out_specs=P(None, AXES), check_vma=False
    )
```

```python
import functools
import math

import jax
import jax.numpy as jnp
from jax import lax
from jax.experimental import pallas as pl
from jax.experimental.pallas import tpu as pltpu
from jax.sharding import PartitionSpec as P

HEADS = 16
PATCH = 1024
REACH = 256
AXES = ("row", "col")
BF = jnp.bfloat16
F32 = jnp.float32
I32 = jnp.int32
I16 = jnp.int16
VM = pl.BlockSpec(memory_space=pltpu.VMEM)


def dot(a, b):
    return jnp.dot(a, b, preferred_element_type=F32)


def dot_nt(a, b):
    return lax.dot_general(a, b, (((1,), (1,)), ((), ())), preferred_element_type=F32)


def layer_norm(values):
    center = values - jnp.mean(values, axis=-1, keepdims=True)
    spread = jnp.mean(center * center, axis=-1, keepdims=True)
    return center * lax.rsqrt(spread + 1e-05)


def gelu(x):
    half = 0.5 * x
    return half + half * jnp.tanh(x * (0.7978845608028654 + 0.035677408136300125 * (x * x)))


def pick(index, rows, cols, dim):
    grid = lax.broadcasted_iota(I16, (rows, cols), dim)
    if dim == 0:
        index = jnp.broadcast_to(index, (16, cols)).astype(I16)[0:1]
    else:
        index = jnp.broadcast_to(index, (rows, 128)).astype(I16)
        index = jnp.concatenate([index] * (cols // 128), axis=1)
    return jnp.where(grid == index, jnp.ones((), BF), jnp.zeros((), BF))


def column(row):
    return jnp.broadcast_to(row, (128, row.shape[1])).T[:, :1]


def place(device):
    inner = lax.axis_size("col")
    return (device // inner, device % inner)


def greet(me, devices):
    barrier = pltpu.get_barrier_semaphore()

    def signal(k, carry):
        pl.semaphore_signal(
            barrier, inc=1, device_id=place((me + k) % devices),
            device_id_type=pl.DeviceIdType.MESH,
        )
        return carry

    lax.fori_loop(1, devices, signal, 0)
    return lambda: pl.semaphore_wait(barrier, devices - 1)


def ship(src, dst, send_sem, recv_sem, device):
    return pltpu.make_async_remote_copy(
        src_ref=src, dst_ref=dst, send_sem=send_sem, recv_sem=recv_sem,
        device_id=place(device), device_id_type=pl.DeviceIdType.MESH,
    )


def spread(src_ref, dst_ref, send_sems, recv_sems, me, devices):
    def start(k, carry):
        peer = (me + k) % devices
        ship(
            src_ref.at[peer], dst_ref.at[me], send_sems.at[peer], recv_sems.at[me], peer
        ).start()
        return carry

    lax.fori_loop(1, devices, start, 0)


def gather_in(src_ref, dst_ref, send_sems, recv_sems, me, devices):
    def finish(k, carry):
        peer = (me + k) % devices
        ship(
            src_ref.at[peer], dst_ref.at[peer], send_sems.at[peer], recv_sems.at[peer], peer
        ).wait()
        return carry

    lax.fori_loop(1, devices, finish, 0)


def kernel(
    devices, capacity, margin, classes,
    z_ref, coarse_ref, fine_ref, parent_ref, nbr_ref, seg_ref,
    w_parent_ref, w_skip_ref, taps_ref, w_cpe_ref,
    w_qkv_hbm, w_out_hbm, w_up_hbm, w_down_hbm, w_cls_ref,
    out_ref,
    w_qkv_ref, w_out_ref, w_up_ref, w_down_ref,
    pos_ref, got_ref, share_ref, slot_ref, take_ref, par_ref, skip_ref, feat_ref, x_ref, send_ref, recv_ref,
    z_sum_ref, zx_ref, kx_ref, qh_ref, ql_ref, v_ref, fq_ref, s_ref, m_ref, att_ref,
    logit_ref, back_ref, ret_ref, part_ref, home_ref,
    slot_send, slot_recv, feat_send, feat_recv, back_send, back_recv, side_send, side_recv, load_sem,
):
    me = lax.axis_index(AXES)
    entered = greet(me, devices)
    loads = [
        pltpu.make_async_copy(src, dst, load_sem.at[i])
        for i, (src, dst) in enumerate(
            (
                (w_qkv_hbm, w_qkv_ref), (w_out_hbm, w_out_ref),
                (w_up_hbm, w_up_ref), (w_down_hbm, w_down_ref),
            )
        )
    ]
    for load in loads:
        load.start()
    rows, width = fine_ref.shape
    coarse_rows = coarse_ref.shape[0]
    coarse = par_ref.shape[0]
    total = devices * capacity
    head_dim = width // HEADS
    block = 256
    lanes = 128
    per_group = 4
    gw = per_group * head_dim
    after, before = (me + 1) % devices, (me + devices - 1) % devices

    par_ref[margin : margin + coarse_rows, :] = gelu(
        layer_norm(dot(coarse_ref[...], w_parent_ref[...]))
    ).astype(BF)
    entered()
    margins = [
        ship(
            par_ref.at[pl.ds(coarse_rows, margin), :], par_ref.at[pl.ds(0, margin), :],
            side_send.at[0], side_recv.at[0], after,
        ),
        ship(
            par_ref.at[pl.ds(margin, margin), :],
            par_ref.at[pl.ds(margin + coarse_rows, margin), :],
            side_send.at[1], side_recv.at[1], before,
        ),
    ]
    for move in margins:
        move.start()

    skip_ref[...] = gelu(layer_norm(dot(fine_ref[...], w_skip_ref[...])))

    z = z_ref[...]
    dest = z // rows
    slot = z % rows
    onehot = pick(dest, devices, rows, 0)
    earlier = lax.broadcasted_iota(I32, (rows, rows), 0) < lax.broadcasted_iota(I32, (rows, rows), 1)
    ahead_of = dot(onehot, jnp.where(earlier, 1.0, 0.0).astype(BF))
    rank = jnp.sum(ahead_of * onehot.astype(F32), axis=0, keepdims=True).astype(I32)
    pos = dest * capacity + rank
    pos_ref[...] = pos

    code = slot + 1
    part = lax.broadcasted_iota(I32, (16, rows), 0)
    digits = jnp.where(part == 0, code // 32, jnp.where(part == 1, code % 32, 0))
    digits = digits.astype(F32).astype(BF)
    piece = min(512, total)
    for start in range(0, total, piece):
        got = dot_nt(digits, pick(pos - start, piece, rows, 0)).astype(I32)
        got = got[0:1] * 32 + got[1:2] - 1
        for d in range(piece // capacity):
            slot_ref[start // capacity + d] = got[:, d * capacity : (d + 1) * capacity]
    spread(slot_ref, take_ref, slot_send, slot_recv, me, devices)
    take_ref[me] = slot_ref[me]

    base_row = me * coarse_rows - margin
    for move in margins:
        move.wait()

    def join(i):
        base = i * block
        at = slice(base, base + block)
        chosen = dot(pick(column(parent_ref[:, at] - base_row), block, coarse, 1), par_ref[...])
        feat_ref[base + REACH : base + REACH + block, :] = (chosen + skip_ref[at, :]).astype(BF)

    blocks = rows // block
    edges = [
        ship(
            feat_ref.at[pl.ds(rows, REACH), :], feat_ref.at[pl.ds(0, REACH), :],
            side_send.at[2], side_recv.at[2], after,
        ),
        ship(
            feat_ref.at[pl.ds(REACH, REACH), :], feat_ref.at[pl.ds(REACH + rows, REACH), :],
            side_send.at[3], side_recv.at[3], before,
        ),
    ]
    join(blocks - 1)
    edges[0].start()
    join(0)
    edges[1].start()
    for i in range(1, blocks - 1):
        join(i)

    window = block + 2 * REACH

    def conv(i, carry):
        base = pl.multiple_of(i * block, block)
        at = pl.ds(base, block)
        cells = feat_ref[pl.ds(base, window), :]
        offsets = nbr_ref[:, at].T
        here = lax.broadcasted_iota(I32, offsets.shape, 0) + REACH
        source = jnp.where(offsets != REACH + 1, here + offsets, -1)
        acc = jnp.zeros((block, cells.shape[1]), F32)
        for t in range(nbr_ref.shape[0]):
            acc = acc + dot(pick(source[:, t : t + 1], block, window, 1), cells) * taps_ref[t : t + 1, :]
        out = layer_norm(dot(acc.astype(BF), w_cpe_ref[...]))
        center = feat_ref[pl.ds(base + REACH, block), :]
        x_ref[at, :] = (center.astype(F32) + out).astype(BF)
        return carry

    lax.fori_loop(1, blocks - 1, conv, 0)
    for move in edges:
        move.wait()
    lax.fori_loop(0, 2, lambda i, carry: conv(i * (blocks - 1), carry), 0)

    pos = pos_ref[...]
    per = block // capacity
    shares = devices // per
    stride = 2

    def block_of(j):
        half = shares // stride
        shift = jnp.where(j < half, stride * j + 1, stride * (j - half) + 2)
        return (me // per + shift) % shares

    def pack(j, carry):
        b = block_of(j)
        sent = dot(pick(pos - b * block, block, rows, 0), x_ref[...]).astype(BF)
        send_ref[pl.ds(b * per, per)] = sent.reshape(per, capacity, width)

        def start(k, inner):
            peer = b * per + k

            @pl.when(peer != me)
            def _():
                ship(
                    send_ref.at[peer], recv_ref.at[me], feat_send.at[peer], feat_recv.at[me], peer
                ).start()

            return inner

        lax.fori_loop(0, per, start, 0)
        return carry

    lax.fori_loop(0, shares, pack, 0)
    recv_ref[me] = send_ref[me]

    bits = (PATCH - 1).bit_length()
    seg = seg_ref[...] - seg_ref[:, 0:1]
    row = lax.broadcasted_iota(I32, (lanes, rows), 0)
    code = ((seg >> (row >> 1)) & 1) ^ (row & 1)
    fq_ref[...] = jnp.where((row < 2 * bits) & (code == 1), 1.0, 0.0).astype(BF)
    lane = lax.broadcasted_iota(I32, (rows, lanes), 1)
    seg_col = jnp.broadcast_to(seg, (lanes, rows)).T
    code = ((seg_col >> (lane >> 1)) & 1) ^ (lane & 1)
    fk = jnp.where((lane < 2 * bits) & (code == 0), -1e30, 0.0).astype(BF)
    for g in range(HEADS // per_group):
        kx_ref[g, :, 2 * gw : 2 * gw + lanes] = fk


    gather_in(slot_ref, take_ref, slot_send, slot_recv, me, devices)
    for d in range(devices):
        got_ref[:, d * capacity : (d + 1) * capacity] = take_ref[d]
    z_sum_ref[...] = jnp.zeros_like(z_sum_ref)
    for load in loads:
        load.wait()
    for d in range(shares):
        share_ref[d] = got_ref[:, d * block : (d + 1) * block]

    def collect(j, carry):
        b = block_of(shares - 1 - j)

        def finish(k, inner):
            peer = b * per + k

            @pl.when(peer != me)
            def _():
                ship(
                    send_ref.at[peer], recv_ref.at[peer], feat_send.at[peer], feat_recv.at[peer], peer
                ).wait()

            return inner

        lax.fori_loop(0, per, finish, 0)
        came = recv_ref[pl.ds(b * per, per)].reshape(block, width)
        z_sum_ref[...] += dot(pick(share_ref[b], rows, block, 0), came)
        return carry

    lax.fori_loop(0, shares, collect, 0)

    z = z_sum_ref[...]
    zx_ref[...] = z.astype(BF)
    normed = layer_norm(z).astype(BF)
    k = dot(normed, w_qkv_ref[:, width : 2 * width]).astype(BF)
    for g in range(HEADS // per_group):
        part = k[:, g * gw : (g + 1) * gw]
        kx_ref[g, :, 0 : 2 * gw] = jnp.concatenate([part, part], axis=1)
    tn = (((0,), (1,)), ((), ()))
    q = lax.dot_general(w_qkv_ref[:, :width], normed, tn, preferred_element_type=F32)
    q = q.astype(BF).astype(F32) * (head_dim**-0.5 * math.log2(math.e))
    high = q.astype(BF)
    qh_ref[...] = high
    ql_ref[...] = (q - high.astype(F32)).astype(BF)
    v = lax.dot_general(w_qkv_ref[:, 2 * width :], normed, tn, preferred_element_type=F32)
    v_ref[...] = v.astype(BF)

    qb = 256
    units = rows // qb
    heads_a_step = 4
    ahead = 2
    slots = 4
    row_head = lax.broadcasted_iota(I32, (gw, qb), 0) // head_dim

    def weights(h, b):
        cols = slice(b * qb, (b + 1) * qb)
        at = pl.ds(pl.multiple_of((h // per_group) * gw, gw), gw)
        mine = row_head == h % per_group
        zero = jnp.zeros((), BF)
        return jnp.concatenate(
            [
                jnp.where(mine, qh_ref[at, cols], zero),
                jnp.where(mine, ql_ref[at, cols], zero),
                fq_ref[:, cols],
            ],
            axis=0,
        )

    def score(h, b, slot):
        w = weights(h, b)
        top = None
        for start in range(0, rows, 512):
            s = dot(kx_ref[h // per_group, start : start + 512, :], w)
            s_ref[slot, start : start + 512, :] = s
            part = jnp.max(s.reshape(512 // 8, 8, qb), axis=0)
            top = part if top is None else jnp.maximum(top, part)
        m_ref[slot] = top

    for u in range(ahead):
        score(u // units, u % units, u % slots)

    def step(i, carry):
        for u in range(heads_a_step * units):
            h, b, cur = i * heads_a_step + u // units, u % units, u % slots
            nxt = u + ahead
            top = jnp.max(m_ref[cur], axis=0, keepdims=True)
            score(
                jnp.minimum(i * heads_a_step + nxt // units, HEADS - 1), nxt % units, nxt % slots
            )
            own = pl.ds(pl.multiple_of(h * head_dim, head_dim), head_dim)
            values = jnp.concatenate([v_ref[own, :], jnp.ones((head_dim, rows), BF)], axis=0)
            acc = None
            for c in range(rows // block):
                at = slice(c * block, (c + 1) * block)
                probs = jnp.exp2(s_ref[cur, at, :] - top).astype(BF)
                part = dot(values[:, at], probs)
                acc = part if acc is None else acc + part
            att = acc[:head_dim] / acc[head_dim : head_dim + 1]
            att_ref[own, b * qb : (b + 1) * qb] = att.astype(BF)
        return carry

    lax.fori_loop(0, HEADS // heads_a_step, step, 0)

    logit_ref[...] = jnp.zeros_like(logit_ref)
    o = lax.dot_general(
        att_ref[...], w_out_ref[...], (((0,), (0,)), ((), ())), preferred_element_type=F32
    ).astype(BF)
    x_two = zx_ref[...].astype(F32) + o.astype(F32)
    hidden = gelu(dot(layer_norm(x_two).astype(BF), w_up_ref[...]).astype(BF))
    x_three = x_two + dot(hidden, w_down_ref[...])
    logit_ref[0:classes, :] = dot_nt(w_cls_ref[...], layer_norm(x_three).astype(BF))

    logits = logit_ref[...]
    high = logits.astype(BF)
    low = (logits - high.astype(F32)).astype(BF)
    both = jnp.concatenate([high, low], axis=0)
    half = high.shape[0]

    def give(j, carry):
        b = block_of(j)
        got = dot(both, pick(share_ref[b], rows, block, 0)).astype(BF)
        for d in range(per):
            at = slice(d * capacity, (d + 1) * capacity)
            back_ref[b * per + d] = jnp.concatenate([got[:half, at], got[half:, at]], axis=1)

        def start(k, inner):
            peer = b * per + k

            @pl.when(peer != me)
            def _():
                ship(
                    back_ref.at[peer], ret_ref.at[me], back_send.at[peer], back_recv.at[me], peer
                ).start()

            return inner

        lax.fori_loop(0, per, start, 0)
        return carry

    lax.fori_loop(0, shares, give, 0)
    ret_ref[me] = back_ref[me]
    home_ref[...] = jnp.zeros_like(home_ref)

    def take(j, carry):
        b = block_of(shares - 1 - j)

        def finish(k, inner):
            peer = b * per + k

            @pl.when(peer != me)
            def _():
                ship(
                    back_ref.at[peer], ret_ref.at[peer], back_send.at[peer], back_recv.at[peer], peer
                ).wait()

            return inner

        lax.fori_loop(0, per, finish, 0)
        for d in range(per):
            came = ret_ref[b * per + d]
            at = slice(d * capacity, (d + 1) * capacity)
            part_ref[0:half, at] = came[:, 0:capacity]
            part_ref[half : 2 * half, at] = came[:, capacity : 2 * capacity]
        home_ref[...] += dot(part_ref[...], pick(pos_ref[...] - b * block, block, rows, 0))
        return carry

    lax.fori_loop(0, shares, take, 0)
    out_ref[...] = home_ref[0:classes, :] + home_ref[half : half + classes, :]


def local(
    coarse_feats,
    fine_feats,
    parent_index,
    nbr_offset,
    z_position,
    segment_id,
    w_parent,
    w_skip,
    conv_taps,
    w_cpe,
    w_qkv,
    w_out,
    w_up,
    w_down,
    w_cls,
):
    fine_rows, width = fine_feats.shape
    coarse_rows = coarse_feats.shape[0]
    devices = lax.axis_size(AXES)
    capacity = 2 * fine_rows // devices
    total = devices * capacity
    assert fine_rows == PATCH

    margin = coarse_rows // 2
    lanes = 128
    classes = w_cls.shape[0]
    half = -(-classes // 16) * 16
    pair = pltpu.SemaphoreType.DMA((devices,))
    side = pltpu.SemaphoreType.DMA((4,))
    return pl.pallas_call(
        functools.partial(kernel, devices, capacity, margin, classes),
        out_shape=jax.ShapeDtypeStruct((classes, fine_rows), F32),
        in_specs=[VM] * 10 + [pl.BlockSpec(memory_space=pl.ANY)] * 4 + [VM],
        out_specs=VM,
        scratch_shapes=[
            *[pltpu.VMEM(w.shape, w.dtype) for w in (w_qkv, w_out, w_up, w_down)],
            pltpu.VMEM((1, fine_rows), I32),
            pltpu.VMEM((1, total), I32),
            pltpu.VMEM((total // 256, 1, 256), I32),
            pltpu.VMEM((devices, 1, capacity), I32),
            pltpu.VMEM((devices, 1, capacity), I32),
            pltpu.VMEM((coarse_rows + 2 * margin, width), BF),
            pltpu.VMEM((fine_rows, width), F32),
            pltpu.VMEM((fine_rows + 2 * REACH, width), BF),
            pltpu.VMEM((fine_rows, width), BF),
            pltpu.VMEM((devices, capacity, width), BF),
            pltpu.VMEM((devices, capacity, width), BF),
            pltpu.VMEM((fine_rows, width), F32),
            pltpu.VMEM((fine_rows, width), BF),
            pltpu.VMEM((HEADS // 4, fine_rows, width // 2 + lanes), BF),
            pltpu.VMEM((width, fine_rows), BF),
            pltpu.VMEM((width, fine_rows), BF),
            pltpu.VMEM((width, fine_rows), BF),
            pltpu.VMEM((lanes, fine_rows), BF),
            pltpu.VMEM((4, fine_rows, 256), F32),
            pltpu.VMEM((4, 8, 256), F32),
            pltpu.VMEM((width, fine_rows), BF),
            pltpu.VMEM((half, fine_rows), F32),
            pltpu.VMEM((devices, half, 2 * capacity), BF),
            pltpu.VMEM((devices, half, 2 * capacity), BF),
            pltpu.VMEM((2 * half, 256), BF),
            pltpu.VMEM((2 * half, fine_rows), F32),
            pair, pair, pair, pair, pair, pair, side, side, side,
        ],
        compiler_params=pltpu.CompilerParams(
            collective_id=0, has_side_effects=True, vmem_limit_bytes=60 * 2**20
        ),
    )(
        z_position.reshape(1, fine_rows), coarse_feats, fine_feats,
        parent_index.reshape(1, fine_rows), nbr_offset, segment_id.reshape(1, fine_rows),
        w_parent, w_skip, conv_taps, w_cpe, w_qkv, w_out, w_up, w_down, w_cls,
    )


def solution(mesh):
    rows = P(AXES, None)
    flat = P(AXES)
    placed = (rows, rows, flat, P(None, AXES), flat, flat) + (P(),) * 9
    return jax.shard_map(
        local, mesh=mesh, in_specs=placed, out_specs=P(None, AXES), check_vma=False
    )
```

```python
import functools
import math

import jax
import jax.numpy as jnp
from jax import lax
from jax.experimental import pallas as pl
from jax.experimental.pallas import tpu as pltpu
from jax.sharding import PartitionSpec as P

HEADS = 16
PATCH = 1024
REACH = 256
AXES = ("row", "col")
BF = jnp.bfloat16
F32 = jnp.float32
I32 = jnp.int32
I16 = jnp.int16
VM = pl.BlockSpec(memory_space=pltpu.VMEM)


def dot(a, b):
    return jnp.dot(a, b, preferred_element_type=F32)


def dot_nt(a, b):
    return lax.dot_general(a, b, (((1,), (1,)), ((), ())), preferred_element_type=F32)


def layer_norm(values):
    center = values - jnp.mean(values, axis=-1, keepdims=True)
    spread = jnp.mean(center * center, axis=-1, keepdims=True)
    return center * lax.rsqrt(spread + 1e-05)


def gelu(x):
    half = 0.5 * x
    return half + half * jnp.tanh(x * (0.7978845608028654 + 0.035677408136300125 * (x * x)))


def pick(index, rows, cols, dim):
    grid = lax.broadcasted_iota(I16, (rows, cols), dim)
    if dim == 0:
        index = jnp.broadcast_to(index, (16, cols)).astype(I16)[0:1]
    else:
        index = jnp.broadcast_to(index, (rows, 128)).astype(I16)
        index = jnp.concatenate([index] * (cols // 128), axis=1)
    return jnp.where(grid == index, jnp.ones((), BF), jnp.zeros((), BF))


def column(row):
    return jnp.broadcast_to(row, (128, row.shape[1])).T[:, :1]


def place(device):
    inner = lax.axis_size("col")
    return (device // inner, device % inner)


def greet(me, devices):
    barrier = pltpu.get_barrier_semaphore()

    def signal(k, carry):
        pl.semaphore_signal(
            barrier, inc=1, device_id=place((me + k) % devices),
            device_id_type=pl.DeviceIdType.MESH,
        )
        return carry

    lax.fori_loop(1, devices, signal, 0)
    return lambda: pl.semaphore_wait(barrier, devices - 1)


def ship(src, dst, send_sem, recv_sem, device):
    return pltpu.make_async_remote_copy(
        src_ref=src, dst_ref=dst, send_sem=send_sem, recv_sem=recv_sem,
        device_id=place(device), device_id_type=pl.DeviceIdType.MESH,
    )


def spread(src_ref, dst_ref, send_sems, recv_sems, me, devices):
    def start(k, carry):
        peer = (me + k) % devices
        ship(
            src_ref.at[peer], dst_ref.at[me], send_sems.at[peer], recv_sems.at[me], peer
        ).start()
        return carry

    lax.fori_loop(1, devices, start, 0)


def gather_in(src_ref, dst_ref, send_sems, recv_sems, me, devices):
    def finish(k, carry):
        peer = (me + k) % devices
        ship(
            src_ref.at[peer], dst_ref.at[peer], send_sems.at[peer], recv_sems.at[peer], peer
        ).wait()
        return carry

    lax.fori_loop(1, devices, finish, 0)


def kernel(
    devices, capacity, margin, classes,
    z_hbm, coarse_hbm, fine_hbm, parent_hbm, nbr_hbm, seg_hbm,
    w_parent_hbm, w_skip_hbm, taps_hbm, w_cpe_hbm,
    w_qkv_hbm, w_out_hbm, w_up_hbm, w_down_hbm, w_cls_hbm,
    out_ref,
    z_ref, coarse_ref, fine_ref, parent_ref, nbr_ref, seg_ref,
    w_parent_ref, w_skip_ref, taps_ref, w_cpe_ref,
    w_qkv_ref, w_out_ref, w_up_ref, w_down_ref, w_cls_ref,
    pos_ref, got_ref, share_ref, slot_ref, take_ref, par_ref, skip_ref, feat_ref, x_ref, send_ref, recv_ref,
    z_sum_ref, zx_ref, kx_ref, qh_ref, ql_ref, v_ref, fq_ref, s_ref, m_ref, att_ref,
    logit_ref, back_ref, ret_ref, part_ref, home_ref,
    slot_send, slot_recv, feat_send, feat_recv, back_send, back_recv, side_send, side_recv, load_sem,
):
    me = lax.axis_index(AXES)
    entered = greet(me, devices)
    order = (
        (coarse_hbm, coarse_ref), (w_parent_hbm, w_parent_ref),
        (fine_hbm, fine_ref), (w_skip_hbm, w_skip_ref), (z_hbm, z_ref), (parent_hbm, parent_ref),
        (nbr_hbm, nbr_ref), (taps_hbm, taps_ref), (w_cpe_hbm, w_cpe_ref), (seg_hbm, seg_ref),
        (w_qkv_hbm, w_qkv_ref), (w_out_hbm, w_out_ref),
        (w_up_hbm, w_up_ref), (w_down_hbm, w_down_ref), (w_cls_hbm, w_cls_ref),
    )
    loads = [
        pltpu.make_async_copy(src, dst, load_sem.at[i]) for i, (src, dst) in enumerate(order)
    ]
    for load in loads:
        load.start()
    rows, width = fine_ref.shape
    coarse_rows = coarse_ref.shape[0]
    coarse = par_ref.shape[0]
    total = devices * capacity
    head_dim = width // HEADS
    block = 256
    lanes = 128
    per_group = 4
    gw = per_group * head_dim
    after, before = (me + 1) % devices, (me + devices - 1) % devices

    for load in loads[:2]:
        load.wait()
    par_ref[margin : margin + coarse_rows, :] = gelu(
        layer_norm(dot(coarse_ref[...], w_parent_ref[...]))
    ).astype(BF)
    entered()
    margins = [
        ship(
            par_ref.at[pl.ds(coarse_rows, margin), :], par_ref.at[pl.ds(0, margin), :],
            side_send.at[0], side_recv.at[0], after,
        ),
        ship(
            par_ref.at[pl.ds(margin, margin), :],
            par_ref.at[pl.ds(margin + coarse_rows, margin), :],
            side_send.at[1], side_recv.at[1], before,
        ),
    ]
    for move in margins:
        move.start()

    for load in loads[2:6]:
        load.wait()
    skip_ref[...] = gelu(layer_norm(dot(fine_ref[...], w_skip_ref[...])))

    z = z_ref[...]
    dest = z // rows
    slot = z % rows
    onehot = pick(dest, devices, rows, 0)
    earlier = lax.broadcasted_iota(I32, (rows, rows), 0) < lax.broadcasted_iota(I32, (rows, rows), 1)
    ahead_of = dot(onehot, jnp.where(earlier, 1.0, 0.0).astype(BF))
    rank = jnp.sum(ahead_of * onehot.astype(F32), axis=0, keepdims=True).astype(I32)
    pos = dest * capacity + rank
    pos_ref[...] = pos

    code = slot + 1
    part = lax.broadcasted_iota(I32, (16, rows), 0)
    digits = jnp.where(part == 0, code // 32, jnp.where(part == 1, code % 32, 0))
    digits = digits.astype(F32).astype(BF)
    piece = min(512, total)
    for start in range(0, total, piece):
        got = dot_nt(digits, pick(pos - start, piece, rows, 0)).astype(I32)
        got = got[0:1] * 32 + got[1:2] - 1
        for d in range(piece // capacity):
            slot_ref[start // capacity + d] = got[:, d * capacity : (d + 1) * capacity]
    spread(slot_ref, take_ref, slot_send, slot_recv, me, devices)
    take_ref[me] = slot_ref[me]

    base_row = me * coarse_rows - margin
    for move in margins:
        move.wait()

    def join(i):
        base = i * block
        at = slice(base, base + block)
        chosen = dot(pick(column(parent_ref[:, at] - base_row), block, coarse, 1), par_ref[...])
        feat_ref[base + REACH : base + REACH + block, :] = (chosen + skip_ref[at, :]).astype(BF)

    blocks = rows // block
    edges = [
        ship(
            feat_ref.at[pl.ds(rows, REACH), :], feat_ref.at[pl.ds(0, REACH), :],
            side_send.at[2], side_recv.at[2], after,
        ),
        ship(
            feat_ref.at[pl.ds(REACH, REACH), :], feat_ref.at[pl.ds(REACH + rows, REACH), :],
            side_send.at[3], side_recv.at[3], before,
        ),
    ]
    join(blocks - 1)
    edges[0].start()
    join(0)
    edges[1].start()
    for i in range(1, blocks - 1):
        join(i)

    window = block + 2 * REACH
    for load in loads[6:9]:
        load.wait()

    def conv(i, carry):
        base = pl.multiple_of(i * block, block)
        at = pl.ds(base, block)
        cells = feat_ref[pl.ds(base, window), :]
        offsets = nbr_ref[:, at].T
        here = lax.broadcasted_iota(I32, offsets.shape, 0) + REACH
        source = jnp.where(offsets != REACH + 1, here + offsets, -1)
        middle = nbr_ref.shape[0] // 2
        center = feat_ref[pl.ds(base + REACH, block), :].astype(F32)
        acc = center * taps_ref[middle : middle + 1, :]
        for t in range(nbr_ref.shape[0]):
            if t == middle:
                continue
            acc = acc + dot(pick(source[:, t : t + 1], block, window, 1), cells) * taps_ref[t : t + 1, :]
        out = layer_norm(dot(acc.astype(BF), w_cpe_ref[...]))
        x_ref[at, :] = (center + out).astype(BF)
        return carry

    lax.fori_loop(1, blocks - 1, conv, 0)
    for move in edges:
        move.wait()
    lax.fori_loop(0, 2, lambda i, carry: conv(i * (blocks - 1), carry), 0)

    pos = pos_ref[...]
    per = block // capacity
    shares = devices // per
    stride = 2

    def block_of(j):
        half = shares // stride
        shift = jnp.where(j < half, stride * j + 1, stride * (j - half) + 2)
        return (me // per + shift) % shares

    def pack(j, carry):
        b = block_of(j)
        sent = dot(pick(pos - b * block, block, rows, 0), x_ref[...]).astype(BF)
        send_ref[pl.ds(b * per, per)] = sent.reshape(per, capacity, width)

        def start(k, inner):
            peer = b * per + k

            @pl.when(peer != me)
            def _():
                ship(
                    send_ref.at[peer], recv_ref.at[me], feat_send.at[peer], feat_recv.at[me], peer
                ).start()

            return inner

        lax.fori_loop(0, per, start, 0)
        return carry

    lax.fori_loop(0, shares, pack, 0)
    recv_ref[me] = send_ref[me]

    for load in loads[9:]:
        load.wait()
    bits = (PATCH - 1).bit_length()
    seg = seg_ref[...] - seg_ref[:, 0:1]
    row = lax.broadcasted_iota(I32, (lanes, rows), 0)
    code = ((seg >> (row >> 1)) & 1) ^ (row & 1)
    fq_ref[...] = jnp.where((row < 2 * bits) & (code == 1), 1.0, 0.0).astype(BF)
    lane = lax.broadcasted_iota(I32, (rows, lanes), 1)
    seg_col = jnp.broadcast_to(seg, (lanes, rows)).T
    code = ((seg_col >> (lane >> 1)) & 1) ^ (lane & 1)
    fk = jnp.where((lane < 2 * bits) & (code == 0), -1e30, 0.0).astype(BF)
    for g in range(HEADS // per_group):
        kx_ref[g, :, 2 * gw : 2 * gw + lanes] = fk


    gather_in(slot_ref, take_ref, slot_send, slot_recv, me, devices)
    for d in range(devices):
        got_ref[:, d * capacity : (d + 1) * capacity] = take_ref[d]
    z_sum_ref[...] = jnp.zeros_like(z_sum_ref)
    for d in range(shares):
        share_ref[d] = got_ref[:, d * block : (d + 1) * block]

    def collect(j, carry):
        b = block_of(shares - 1 - j)

        def finish(k, inner):
            peer = b * per + k

            @pl.when(peer != me)
            def _():
                ship(
                    send_ref.at[peer], recv_ref.at[peer], feat_send.at[peer], feat_recv.at[peer], peer
                ).wait()

            return inner

        lax.fori_loop(0, per, finish, 0)
        came = recv_ref[pl.ds(b * per, per)].reshape(block, width)
        z_sum_ref[...] += dot(pick(share_ref[b], rows, block, 0), came)
        return carry

    lax.fori_loop(0, shares, collect, 0)

    z = z_sum_ref[...]
    zx_ref[...] = z.astype(BF)
    normed = layer_norm(z).astype(BF)
    k = dot(normed, w_qkv_ref[:, width : 2 * width]).astype(BF)
    for g in range(HEADS // per_group):
        part = k[:, g * gw : (g + 1) * gw]
        kx_ref[g, :, 0 : 2 * gw] = jnp.concatenate([part, part], axis=1)
    tn = (((0,), (1,)), ((), ()))
    q = lax.dot_general(w_qkv_ref[:, :width], normed, tn, preferred_element_type=F32)
    q = q.astype(BF).astype(F32) * (head_dim**-0.5 * math.log2(math.e))
    high = q.astype(BF)
    qh_ref[...] = high
    ql_ref[...] = (q - high.astype(F32)).astype(BF)
    v = lax.dot_general(w_qkv_ref[:, 2 * width :], normed, tn, preferred_element_type=F32)
    v_ref[...] = v.astype(BF)

    qb = 256
    units = rows // qb
    heads_a_step = 4
    ahead = 2
    slots = 4
    row_head = lax.broadcasted_iota(I32, (gw, qb), 0) // head_dim

    def weights(h, b):
        cols = slice(b * qb, (b + 1) * qb)
        at = pl.ds(pl.multiple_of((h // per_group) * gw, gw), gw)
        mine = row_head == h % per_group
        zero = jnp.zeros((), BF)
        return jnp.concatenate(
            [
                jnp.where(mine, qh_ref[at, cols], zero),
                jnp.where(mine, ql_ref[at, cols], zero),
                fq_ref[:, cols],
            ],
            axis=0,
        )

    def score(h, b, slot):
        w = weights(h, b)
        top = None
        for start in range(0, rows, 512):
            s = dot(kx_ref[h // per_group, start : start + 512, :], w)
            s_ref[slot, start : start + 512, :] = s
            part = jnp.max(s.reshape(512 // 8, 8, qb), axis=0)
            top = part if top is None else jnp.maximum(top, part)
        m_ref[slot] = top

    for u in range(ahead):
        score(u // units, u % units, u % slots)

    def step(i, carry):
        for u in range(heads_a_step * units):
            h, b, cur = i * heads_a_step + u // units, u % units, u % slots
            nxt = u + ahead
            top = jnp.max(m_ref[cur], axis=0, keepdims=True)
            score(
                jnp.minimum(i * heads_a_step + nxt // units, HEADS - 1), nxt % units, nxt % slots
            )
            own = pl.ds(pl.multiple_of(h * head_dim, head_dim), head_dim)
            values = jnp.concatenate([v_ref[own, :], jnp.ones((head_dim, rows), BF)], axis=0)
            acc = None
            for c in range(rows // block):
                at = slice(c * block, (c + 1) * block)
                probs = jnp.exp2(s_ref[cur, at, :] - top).astype(BF)
                part = dot(values[:, at], probs)
                acc = part if acc is None else acc + part
            att = acc[:head_dim] / acc[head_dim : head_dim + 1]
            att_ref[own, b * qb : (b + 1) * qb] = att.astype(BF)
        return carry

    lax.fori_loop(0, HEADS // heads_a_step, step, 0)

    logit_ref[...] = jnp.zeros_like(logit_ref)
    o = lax.dot_general(
        att_ref[...], w_out_ref[...], (((0,), (0,)), ((), ())), preferred_element_type=F32
    ).astype(BF)
    x_two = zx_ref[...].astype(F32) + o.astype(F32)
    hidden = gelu(dot(layer_norm(x_two).astype(BF), w_up_ref[...]).astype(BF))
    x_three = x_two + dot(hidden, w_down_ref[...])
    logit_ref[0:classes, :] = dot_nt(w_cls_ref[...], layer_norm(x_three).astype(BF))

    logits = logit_ref[...]
    high = logits.astype(BF)
    low = (logits - high.astype(F32)).astype(BF)
    both = jnp.concatenate([high, low], axis=0)
    half = high.shape[0]

    piece = min(512, total // 2)
    peers = devices // 2
    for side in range(2):
        for start in range(side * total // 2, (side + 1) * total // 2, piece):
            got = dot(both, pick(got_ref[:, start : start + piece], rows, piece, 0)).astype(BF)
            for d in range(piece // capacity):
                at = slice(d * capacity, (d + 1) * capacity)
                back_ref[start // capacity + d] = jnp.concatenate([got[:half, at], got[half:, at]], axis=1)

        def start_back(k, carry):
            peer = side * peers + (me + k) % peers

            @pl.when(peer != me)
            def _():
                ship(
                    back_ref.at[peer], ret_ref.at[me], back_send.at[peer], back_recv.at[me], peer
                ).start()

            return carry

        lax.fori_loop(0, peers, start_back, 0)
    ret_ref[me] = back_ref[me]

    for side in range(2):

        def finish_back(k, carry):
            peer = side * peers + (me + k) % peers

            @pl.when(peer != me)
            def _():
                ship(
                    back_ref.at[peer], ret_ref.at[peer], back_send.at[peer], back_recv.at[peer], peer
                ).wait()

            return carry

        lax.fori_loop(0, peers, finish_back, 0)
        for d in range(peers):
            came = ret_ref[side * peers + d]
            at = slice(d * capacity, (d + 1) * capacity)
            part_ref[0:half, at] = came[:, 0:capacity]
            part_ref[half : 2 * half, at] = came[:, capacity : 2 * capacity]
        found = dot(part_ref[...], pick(pos_ref[...] - side * (total // 2), total // 2, rows, 0))
        if side == 0:
            home_ref[...] = found
        else:
            home_ref[...] += found

    out_ref[...] = home_ref[0:classes, :] + home_ref[half : half + classes, :]


def local(
    coarse_feats,
    fine_feats,
    parent_index,
    nbr_offset,
    z_position,
    segment_id,
    w_parent,
    w_skip,
    conv_taps,
    w_cpe,
    w_qkv,
    w_out,
    w_up,
    w_down,
    w_cls,
):
    fine_rows, width = fine_feats.shape
    coarse_rows = coarse_feats.shape[0]
    devices = lax.axis_size(AXES)
    capacity = 2 * fine_rows // devices
    total = devices * capacity
    assert fine_rows == PATCH

    margin = coarse_rows // 2
    lanes = 128
    classes = w_cls.shape[0]
    half = -(-classes // 16) * 16
    pair = pltpu.SemaphoreType.DMA((devices,))
    side = pltpu.SemaphoreType.DMA((4,))
    operands = (
        z_position.reshape(1, fine_rows), coarse_feats, fine_feats,
        parent_index.reshape(1, fine_rows), nbr_offset, segment_id.reshape(1, fine_rows),
        w_parent, w_skip, conv_taps, w_cpe, w_qkv, w_out, w_up, w_down, w_cls,
    )
    return pl.pallas_call(
        functools.partial(kernel, devices, capacity, margin, classes),
        out_shape=jax.ShapeDtypeStruct((classes, fine_rows), F32),
        in_specs=[pl.BlockSpec(memory_space=pl.ANY)] * len(operands),
        out_specs=VM,
        scratch_shapes=[
            *[pltpu.VMEM(a.shape, a.dtype) for a in operands],
            pltpu.VMEM((1, fine_rows), I32),
            pltpu.VMEM((1, total), I32),
            pltpu.VMEM((total // 256, 1, 256), I32),
            pltpu.VMEM((devices, 1, capacity), I32),
            pltpu.VMEM((devices, 1, capacity), I32),
            pltpu.VMEM((coarse_rows + 2 * margin, width), BF),
            pltpu.VMEM((fine_rows, width), F32),
            pltpu.VMEM((fine_rows + 2 * REACH, width), BF),
            pltpu.VMEM((fine_rows, width), BF),
            pltpu.VMEM((devices, capacity, width), BF),
            pltpu.VMEM((devices, capacity, width), BF),
            pltpu.VMEM((fine_rows, width), F32),
            pltpu.VMEM((fine_rows, width), BF),
            pltpu.VMEM((HEADS // 4, fine_rows, width // 2 + lanes), BF),
            pltpu.VMEM((width, fine_rows), BF),
            pltpu.VMEM((width, fine_rows), BF),
            pltpu.VMEM((width, fine_rows), BF),
            pltpu.VMEM((lanes, fine_rows), BF),
            pltpu.VMEM((4, fine_rows, 256), F32),
            pltpu.VMEM((4, 8, 256), F32),
            pltpu.VMEM((width, fine_rows), BF),
            pltpu.VMEM((half, fine_rows), F32),
            pltpu.VMEM((devices, half, 2 * capacity), BF),
            pltpu.VMEM((devices, half, 2 * capacity), BF),
            pltpu.VMEM((2 * half, total // 2), BF),
            pltpu.VMEM((2 * half, fine_rows), F32),
            pair, pair, pair, pair, pair, pair, side, side,
            pltpu.SemaphoreType.DMA((len(operands),)),
        ],
        compiler_params=pltpu.CompilerParams(
            collective_id=0, has_side_effects=True, vmem_limit_bytes=60 * 2**20
        ),
    )(*operands)


def solution(mesh):
    rows = P(AXES, None)
    flat = P(AXES)
    placed = (rows, rows, flat, P(None, AXES), flat, flat) + (P(),) * 9
    return jax.shard_map(
        local, mesh=mesh, in_specs=placed, out_specs=P(None, AXES), check_vma=False
    )
```

```python
import functools
import math

import jax
import jax.numpy as jnp
from jax import lax
from jax.experimental import pallas as pl
from jax.experimental.pallas import tpu as pltpu
from jax.sharding import PartitionSpec as P

HEADS = 16
PATCH = 1024
REACH = 256
AXES = ("row", "col")
BF = jnp.bfloat16
F32 = jnp.float32
I32 = jnp.int32
I16 = jnp.int16
VM = pl.BlockSpec(memory_space=pltpu.VMEM)


def dot(a, b):
    return jnp.dot(a, b, preferred_element_type=F32)


def dot_nt(a, b):
    return lax.dot_general(a, b, (((1,), (1,)), ((), ())), preferred_element_type=F32)


def layer_norm(values):
    center = values - jnp.mean(values, axis=-1, keepdims=True)
    spread = jnp.mean(center * center, axis=-1, keepdims=True)
    return center * lax.rsqrt(spread + 1e-05)


def gelu(x):
    half = 0.5 * x
    return half + half * jnp.tanh(x * (0.7978845608028654 + 0.035677408136300125 * (x * x)))


def pick(index, rows, cols, dim):
    grid = lax.broadcasted_iota(I16, (rows, cols), dim)
    if dim == 0:
        index = jnp.broadcast_to(index, (16, cols)).astype(I16)[0:1]
    else:
        index = jnp.broadcast_to(index, (rows, 128)).astype(I16)
        index = jnp.concatenate([index] * (cols // 128), axis=1)
    return jnp.where(grid == index, jnp.ones((), BF), jnp.zeros((), BF))


def column(row):
    return jnp.broadcast_to(row, (128, row.shape[1])).T[:, :1]


def place(device):
    inner = lax.axis_size("col")
    return (device // inner, device % inner)


def greet(me, devices):
    barrier = pltpu.get_barrier_semaphore()

    def signal(k, carry):
        pl.semaphore_signal(
            barrier, inc=1, device_id=place((me + k) % devices),
            device_id_type=pl.DeviceIdType.MESH,
        )
        return carry

    lax.fori_loop(1, devices, signal, 0)
    return lambda: pl.semaphore_wait(barrier, devices - 1)


def ship(src, dst, send_sem, recv_sem, device):
    return pltpu.make_async_remote_copy(
        src_ref=src, dst_ref=dst, send_sem=send_sem, recv_sem=recv_sem,
        device_id=place(device), device_id_type=pl.DeviceIdType.MESH,
    )


def spread(src_ref, dst_ref, send_sems, recv_sems, me, devices):
    def start(k, carry):
        peer = (me + k) % devices
        ship(
            src_ref.at[peer], dst_ref.at[me], send_sems.at[peer], recv_sems.at[me], peer
        ).start()
        return carry

    lax.fori_loop(1, devices, start, 0)


def gather_in(src_ref, dst_ref, send_sems, recv_sems, me, devices):
    def finish(k, carry):
        peer = (me + k) % devices
        ship(
            src_ref.at[peer], dst_ref.at[peer], send_sems.at[peer], recv_sems.at[peer], peer
        ).wait()
        return carry

    lax.fori_loop(1, devices, finish, 0)


def kernel(
    devices, capacity, margin, classes,
    z_hbm, coarse_hbm, fine_hbm, parent_hbm, nbr_hbm, seg_hbm,
    w_parent_hbm, w_skip_hbm, taps_hbm, w_cpe_hbm,
    w_qkv_hbm, w_out_hbm, w_up_hbm, w_down_hbm, w_cls_hbm,
    out_ref,
    z_ref, coarse_ref, fine_ref, parent_ref, nbr_ref, seg_ref,
    w_parent_ref, w_skip_ref, taps_ref, w_cpe_ref,
    w_qkv_ref, w_out_ref, w_up_ref, w_down_ref, w_cls_ref,
    pos_ref, got_ref, share_ref, slot_ref, take_ref, par_ref, skip_ref, feat_ref, x_ref, send_ref, recv_ref,
    z_sum_ref, zx_ref, wqv_ref, wk_ref, kx_ref, qh_ref, ql_ref, v_ref, fq_ref, s_ref, m_ref, att_ref,
    logit_ref, back_ref, ret_ref, part_ref, home_ref,
    slot_send, slot_recv, feat_send, feat_recv, back_send, back_recv, side_send, side_recv, load_sem,
):
    me = lax.axis_index(AXES)
    entered = greet(me, devices)
    order = (
        (coarse_hbm, coarse_ref), (w_parent_hbm, w_parent_ref),
        (fine_hbm, fine_ref), (w_skip_hbm, w_skip_ref), (z_hbm, z_ref), (parent_hbm, parent_ref),
        (nbr_hbm, nbr_ref), (taps_hbm, taps_ref), (w_cpe_hbm, w_cpe_ref), (seg_hbm, seg_ref),
        (w_qkv_hbm, w_qkv_ref), (w_out_hbm, w_out_ref),
        (w_up_hbm, w_up_ref), (w_down_hbm, w_down_ref), (w_cls_hbm, w_cls_ref),
    )
    loads = [
        pltpu.make_async_copy(src, dst, load_sem.at[i]) for i, (src, dst) in enumerate(order)
    ]
    for load in loads:
        load.start()
    rows, width = fine_ref.shape
    coarse_rows = coarse_ref.shape[0]
    coarse = par_ref.shape[0]
    total = devices * capacity
    head_dim = width // HEADS
    block = 256
    lanes = 128
    per_group = 4
    gw = per_group * head_dim
    after, before = (me + 1) % devices, (me + devices - 1) % devices

    for load in loads[:2]:
        load.wait()
    par_ref[margin : margin + coarse_rows, :] = gelu(
        layer_norm(dot(coarse_ref[...], w_parent_ref[...]))
    ).astype(BF)
    entered()
    margins = [
        ship(
            par_ref.at[pl.ds(coarse_rows, margin), :], par_ref.at[pl.ds(0, margin), :],
            side_send.at[0], side_recv.at[0], after,
        ),
        ship(
            par_ref.at[pl.ds(margin, margin), :],
            par_ref.at[pl.ds(margin + coarse_rows, margin), :],
            side_send.at[1], side_recv.at[1], before,
        ),
    ]
    for move in margins:
        move.start()

    for load in loads[2:6]:
        load.wait()
    skip_ref[...] = gelu(layer_norm(dot(fine_ref[...], w_skip_ref[...])))

    z = z_ref[...]
    dest = z // rows
    slot = z % rows
    onehot = pick(dest, devices, rows, 0)
    earlier = lax.broadcasted_iota(I32, (rows, rows), 0) < lax.broadcasted_iota(I32, (rows, rows), 1)
    ahead_of = dot(onehot, jnp.where(earlier, 1.0, 0.0).astype(BF))
    rank = jnp.sum(ahead_of * onehot.astype(F32), axis=0, keepdims=True).astype(I32)
    pos = dest * capacity + rank
    pos_ref[...] = pos

    code = slot + 1
    part = lax.broadcasted_iota(I32, (16, rows), 0)
    digits = jnp.where(part == 0, code // 32, jnp.where(part == 1, code % 32, 0))
    digits = digits.astype(F32).astype(BF)
    piece = min(512, total)
    for start in range(0, total, piece):
        got = dot_nt(digits, pick(pos - start, piece, rows, 0)).astype(I32)
        got = got[0:1] * 32 + got[1:2] - 1
        for d in range(piece // capacity):
            slot_ref[start // capacity + d] = got[:, d * capacity : (d + 1) * capacity]
    spread(slot_ref, take_ref, slot_send, slot_recv, me, devices)
    take_ref[me] = slot_ref[me]

    base_row = me * coarse_rows - margin
    for move in margins:
        move.wait()

    def join(i):
        base = i * block
        at = slice(base, base + block)
        chosen = dot(pick(column(parent_ref[:, at] - base_row), block, coarse, 1), par_ref[...])
        feat_ref[base + REACH : base + REACH + block, :] = (chosen + skip_ref[at, :]).astype(BF)

    blocks = rows // block
    edges = [
        ship(
            feat_ref.at[pl.ds(rows, REACH), :], feat_ref.at[pl.ds(0, REACH), :],
            side_send.at[2], side_recv.at[2], after,
        ),
        ship(
            feat_ref.at[pl.ds(REACH, REACH), :], feat_ref.at[pl.ds(REACH + rows, REACH), :],
            side_send.at[3], side_recv.at[3], before,
        ),
    ]
    join(blocks - 1)
    edges[0].start()
    join(0)
    edges[1].start()
    for i in range(1, blocks - 1):
        join(i)

    window = block + 2 * REACH
    for load in loads[6:9]:
        load.wait()

    def conv(i, carry):
        base = pl.multiple_of(i * block, block)
        at = pl.ds(base, block)
        cells = feat_ref[pl.ds(base, window), :]
        offsets = nbr_ref[:, at].T
        here = lax.broadcasted_iota(I32, offsets.shape, 0) + REACH
        source = jnp.where(offsets != REACH + 1, here + offsets, -1)
        middle = nbr_ref.shape[0] // 2
        center = feat_ref[pl.ds(base + REACH, block), :].astype(F32)
        acc = center * taps_ref[middle : middle + 1, :]
        for t in range(nbr_ref.shape[0]):
            if t == middle:
                continue
            acc = acc + dot(pick(source[:, t : t + 1], block, window, 1), cells) * taps_ref[t : t + 1, :]
        out = layer_norm(dot(acc.astype(BF), w_cpe_ref[...]))
        x_ref[at, :] = (center + out).astype(BF)
        return carry

    lax.fori_loop(1, blocks - 1, conv, 0)
    for move in edges:
        move.wait()
    lax.fori_loop(0, 2, lambda i, carry: conv(i * (blocks - 1), carry), 0)

    pos = pos_ref[...]
    per = block // capacity
    shares = devices // per
    stride = 2

    def block_of(j):
        half = shares // stride
        shift = jnp.where(j < half, stride * j + 1, stride * (j - half) + 2)
        return (me // per + shift) % shares

    def pack(j, carry):
        b = block_of(j)
        sent = dot(pick(pos - b * block, block, rows, 0), x_ref[...]).astype(BF)
        send_ref[pl.ds(b * per, per)] = sent.reshape(per, capacity, width)

        def start(k, inner):
            peer = b * per + k

            @pl.when(peer != me)
            def _():
                ship(
                    send_ref.at[peer], recv_ref.at[me], feat_send.at[peer], feat_recv.at[me], peer
                ).start()

            return inner

        lax.fori_loop(0, per, start, 0)
        return carry

    lax.fori_loop(0, shares, pack, 0)
    recv_ref[me] = send_ref[me]

    for load in loads[9:]:
        load.wait()
    bits = (PATCH - 1).bit_length()
    seg = seg_ref[...] - seg_ref[:, 0:1]
    row = lax.broadcasted_iota(I32, (lanes, rows), 0)
    code = ((seg >> (row >> 1)) & 1) ^ (row & 1)
    fq_ref[...] = jnp.where((row < 2 * bits) & (code == 1), 1.0, 0.0).astype(BF)
    lane = lax.broadcasted_iota(I32, (rows, lanes), 1)
    seg_col = jnp.broadcast_to(seg, (lanes, rows)).T
    code = ((seg_col >> (lane >> 1)) & 1) ^ (lane & 1)
    fk = jnp.where((lane < 2 * bits) & (code == 0), -1e30, 0.0).astype(BF)
    for g in range(HEADS // per_group):
        kx_ref[g, :, 2 * gw : 2 * gw + lanes] = fk


    gather_in(slot_ref, take_ref, slot_send, slot_recv, me, devices)
    for d in range(devices):
        got_ref[:, d * capacity : (d + 1) * capacity] = take_ref[d]
    wqv_ref[0:width, :] = w_qkv_ref[:, 0:width].astype(F32).T.astype(BF)
    wqv_ref[width : 2 * width, :] = w_qkv_ref[:, 2 * width :].astype(F32).T.astype(BF)
    for g in range(HEADS // per_group):
        part = w_qkv_ref[:, width + g * gw : width + (g + 1) * gw]
        wk_ref[:, 2 * g * gw : 2 * (g + 1) * gw] = jnp.concatenate([part, part], axis=1)
    z_sum_ref[...] = jnp.zeros_like(z_sum_ref)
    for d in range(shares):
        share_ref[d] = got_ref[:, d * block : (d + 1) * block]

    def collect(j, carry):
        b = block_of(shares - 1 - j)

        def finish(k, inner):
            peer = b * per + k

            @pl.when(peer != me)
            def _():
                ship(
                    send_ref.at[peer], recv_ref.at[peer], feat_send.at[peer], feat_recv.at[peer], peer
                ).wait()

            return inner

        lax.fori_loop(0, per, finish, 0)
        came = recv_ref[pl.ds(b * per, per)].reshape(block, width)
        z_sum_ref[...] += dot(pick(share_ref[b], rows, block, 0), came)
        return carry

    lax.fori_loop(0, shares, collect, 0)

    z = z_sum_ref[...]
    zx_ref[...] = z.astype(BF)
    normed = layer_norm(z).astype(BF)
    for g in range(0, HEADS // per_group, 2):
        k = dot(normed, wk_ref[:, 2 * g * gw : 2 * (g + 2) * gw]).astype(BF)
        kx_ref[g, :, 0 : 2 * gw] = k[:, : 2 * gw]
        kx_ref[g + 1, :, 0 : 2 * gw] = k[:, 2 * gw :]
    qv = dot_nt(wqv_ref[...], normed)
    q = qv[:width].astype(BF).astype(F32) * (head_dim**-0.5 * math.log2(math.e))
    high = q.astype(BF)
    qh_ref[...] = high
    ql_ref[...] = (q - high.astype(F32)).astype(BF)
    v_ref[...] = qv[width:].astype(BF)

    qb = 256
    units = rows // qb
    heads_a_step = 4
    ahead = 2
    slots = 4
    row_head = lax.broadcasted_iota(I32, (gw, qb), 0) // head_dim

    def weights(h, b):
        cols = slice(b * qb, (b + 1) * qb)
        at = pl.ds(pl.multiple_of((h // per_group) * gw, gw), gw)
        mine = row_head == h % per_group
        zero = jnp.zeros((), BF)
        return jnp.concatenate(
            [
                jnp.where(mine, qh_ref[at, cols], zero),
                jnp.where(mine, ql_ref[at, cols], zero),
                fq_ref[:, cols],
            ],
            axis=0,
        )

    span = 512

    def score(h, b, slot, w, start, top):
        s = dot(kx_ref[h // per_group, start : start + span, :], w)
        s_ref[slot, start : start + span, :] = s
        part = jnp.max(s.reshape(span // 8, 8, qb), axis=0)
        return part if top is None else jnp.maximum(top, part)

    for u in range(ahead):
        w, top = weights(u // units, u % units), None
        for start in range(0, rows, span):
            top = score(u // units, u % units, u % slots, w, start, top)
        m_ref[u % slots] = top

    def step(i, carry):
        for u in range(heads_a_step * units):
            h, b, cur = i * heads_a_step + u // units, u % units, u % slots
            nxt = u + ahead
            later = jnp.minimum(i * heads_a_step + nxt // units, HEADS - 1)
            w, top = weights(later, nxt % units), None
            peak = jnp.max(m_ref[cur], axis=0, keepdims=True)
            own = pl.ds(pl.multiple_of(h * head_dim, head_dim), head_dim)
            values = jnp.concatenate([v_ref[own, :], jnp.ones((head_dim, rows), BF)], axis=0)
            acc = None
            for start in range(0, rows, span):
                top = score(later, nxt % units, nxt % slots, w, start, top)
                for c in range(start, start + span, block):
                    probs = jnp.exp2(s_ref[cur, c : c + block, :] - peak).astype(BF)
                    part = dot(values[:, c : c + block], probs)
                    acc = part if acc is None else acc + part
            m_ref[nxt % slots] = top
            att = acc[:head_dim] / acc[head_dim : head_dim + 1]
            att_ref[own, b * qb : (b + 1) * qb] = att.astype(BF)
        return carry

    lax.fori_loop(0, HEADS // heads_a_step, step, 0)

    logit_ref[...] = jnp.zeros_like(logit_ref)
    o = lax.dot_general(
        att_ref[...], w_out_ref[...], (((0,), (0,)), ((), ())), preferred_element_type=F32
    ).astype(BF)
    x_two = zx_ref[...].astype(F32) + o.astype(F32)
    hidden = gelu(dot(layer_norm(x_two).astype(BF), w_up_ref[...]).astype(BF))
    x_three = x_two + dot(hidden, w_down_ref[...])
    logit_ref[0:classes, :] = dot_nt(w_cls_ref[...], layer_norm(x_three).astype(BF))

    logits = logit_ref[...].astype(BF)
    piece = min(512, total // 2)
    peers = devices // 2
    for side in range(2):
        for start in range(side * total // 2, (side + 1) * total // 2, piece):
            got = dot(logits, pick(got_ref[:, start : start + piece], rows, piece, 0)).astype(BF)
            for d in range(piece // capacity):
                at = slice(d * capacity, (d + 1) * capacity)
                back_ref[start // capacity + d] = got[:, at]

        def start_back(k, carry):
            peer = side * peers + (me + k) % peers

            @pl.when(peer != me)
            def _():
                ship(
                    back_ref.at[peer], ret_ref.at[me], back_send.at[peer], back_recv.at[me], peer
                ).start()

            return carry

        lax.fori_loop(0, peers, start_back, 0)
    ret_ref[me] = back_ref[me]

    for side in range(2):

        def finish_back(k, carry):
            peer = side * peers + (me + k) % peers

            @pl.when(peer != me)
            def _():
                ship(
                    back_ref.at[peer], ret_ref.at[peer], back_send.at[peer], back_recv.at[peer], peer
                ).wait()

            return carry

        lax.fori_loop(0, peers, finish_back, 0)
        for d in range(peers):
            part_ref[:, d * capacity : (d + 1) * capacity] = ret_ref[side * peers + d]
        found = dot(part_ref[...], pick(pos_ref[...] - side * (total // 2), total // 2, rows, 0))
        if side == 0:
            home_ref[...] = found
        else:
            home_ref[...] += found

    out_ref[...] = home_ref[0:classes, :]


def local(
    coarse_feats,
    fine_feats,
    parent_index,
    nbr_offset,
    z_position,
    segment_id,
    w_parent,
    w_skip,
    conv_taps,
    w_cpe,
    w_qkv,
    w_out,
    w_up,
    w_down,
    w_cls,
):
    fine_rows, width = fine_feats.shape
    coarse_rows = coarse_feats.shape[0]
    devices = lax.axis_size(AXES)
    capacity = 2 * fine_rows // devices
    total = devices * capacity
    assert fine_rows == PATCH

    margin = coarse_rows // 2
    lanes = 128
    classes = w_cls.shape[0]
    half = -(-classes // 16) * 16
    pair = pltpu.SemaphoreType.DMA((devices,))
    side = pltpu.SemaphoreType.DMA((4,))
    operands = (
        z_position.reshape(1, fine_rows), coarse_feats, fine_feats,
        parent_index.reshape(1, fine_rows), nbr_offset, segment_id.reshape(1, fine_rows),
        w_parent, w_skip, conv_taps, w_cpe, w_qkv, w_out, w_up, w_down, w_cls,
    )
    return pl.pallas_call(
        functools.partial(kernel, devices, capacity, margin, classes),
        out_shape=jax.ShapeDtypeStruct((classes, fine_rows), F32),
        in_specs=[pl.BlockSpec(memory_space=pl.ANY)] * len(operands),
        out_specs=VM,
        scratch_shapes=[
            *[pltpu.VMEM(a.shape, a.dtype) for a in operands],
            pltpu.VMEM((1, fine_rows), I32),
            pltpu.VMEM((1, total), I32),
            pltpu.VMEM((total // 256, 1, 256), I32),
            pltpu.VMEM((devices, 1, capacity), I32),
            pltpu.VMEM((devices, 1, capacity), I32),
            pltpu.VMEM((coarse_rows + 2 * margin, width), BF),
            pltpu.VMEM((fine_rows, width), F32),
            pltpu.VMEM((fine_rows + 2 * REACH, width), BF),
            pltpu.VMEM((fine_rows, width), BF),
            pltpu.VMEM((devices, capacity, width), BF),
            pltpu.VMEM((devices, capacity, width), BF),
            pltpu.VMEM((fine_rows, width), F32),
            pltpu.VMEM((fine_rows, width), BF),
            pltpu.VMEM((2 * width, width), BF),
            pltpu.VMEM((width, 2 * width), BF),
            pltpu.VMEM((HEADS // 4, fine_rows, width // 2 + lanes), BF),
            pltpu.VMEM((width, fine_rows), BF),
            pltpu.VMEM((width, fine_rows), BF),
            pltpu.VMEM((width, fine_rows), BF),
            pltpu.VMEM((lanes, fine_rows), BF),
            pltpu.VMEM((4, fine_rows, 256), F32),
            pltpu.VMEM((4, 8, 256), F32),
            pltpu.VMEM((width, fine_rows), BF),
            pltpu.VMEM((half, fine_rows), F32),
            pltpu.VMEM((devices, half, capacity), BF),
            pltpu.VMEM((devices, half, capacity), BF),
            pltpu.VMEM((half, total // 2), BF),
            pltpu.VMEM((half, fine_rows), F32),
            pair, pair, pair, pair, pair, pair, side, side,
            pltpu.SemaphoreType.DMA((len(operands),)),
        ],
        compiler_params=pltpu.CompilerParams(
            collective_id=0, has_side_effects=True, vmem_limit_bytes=60 * 2**20
        ),
    )(*operands)


def solution(mesh):
    rows = P(AXES, None)
    flat = P(AXES)
    placed = (rows, rows, flat, P(None, AXES), flat, flat) + (P(),) * 9
    return jax.shard_map(
        local, mesh=mesh, in_specs=placed, out_specs=P(None, AXES), check_vma=False
    )
```

```python
import functools
import math

import jax
import jax.numpy as jnp
from jax import lax
from jax.experimental import pallas as pl
from jax.experimental.pallas import tpu as pltpu
from jax.sharding import PartitionSpec as P

HEADS = 16
PATCH = 1024
REACH = 256
AXES = ("row", "col")
BF = jnp.bfloat16
F32 = jnp.float32
I32 = jnp.int32
I16 = jnp.int16
VM = pl.BlockSpec(memory_space=pltpu.VMEM)


def dot(a, b):
    return jnp.dot(a, b, preferred_element_type=F32)


def dot_nt(a, b):
    return lax.dot_general(a, b, (((1,), (1,)), ((), ())), preferred_element_type=F32)


def layer_norm(values):
    center = values - jnp.mean(values, axis=-1, keepdims=True)
    spread = jnp.mean(center * center, axis=-1, keepdims=True)
    return center * lax.rsqrt(spread + 1e-05)


def gelu(x):
    half = 0.5 * x
    return half + half * jnp.tanh(x * (0.7978845608028654 + 0.035677408136300125 * (x * x)))


def pick(index, rows, cols, dim):
    grid = lax.broadcasted_iota(I16, (rows, cols), dim)
    if dim == 0:
        index = jnp.broadcast_to(index, (16, cols)).astype(I16)[0:1]
    else:
        index = jnp.broadcast_to(index, (rows, 128)).astype(I16)
        index = jnp.concatenate([index] * (cols // 128), axis=1)
    return jnp.where(grid == index, jnp.ones((), BF), jnp.zeros((), BF))


def column(row):
    return jnp.broadcast_to(row, (128, row.shape[1])).T[:, :1]


def place(device):
    inner = lax.axis_size("col")
    return (device // inner, device % inner)


def greet(me, devices):
    barrier = pltpu.get_barrier_semaphore()

    def signal(k, carry):
        pl.semaphore_signal(
            barrier, inc=1, device_id=place((me + k) % devices),
            device_id_type=pl.DeviceIdType.MESH,
        )
        return carry

    lax.fori_loop(1, devices, signal, 0)
    return lambda: pl.semaphore_wait(barrier, devices - 1)


def ship(src, dst, send_sem, recv_sem, device):
    return pltpu.make_async_remote_copy(
        src_ref=src, dst_ref=dst, send_sem=send_sem, recv_sem=recv_sem,
        device_id=place(device), device_id_type=pl.DeviceIdType.MESH,
    )


def spread(src_ref, dst_ref, send_sems, recv_sems, me, devices):
    def start(k, carry):
        peer = (me + k) % devices
        ship(
            src_ref.at[peer], dst_ref.at[me], send_sems.at[peer], recv_sems.at[me], peer
        ).start()
        return carry

    lax.fori_loop(1, devices, start, 0)


def gather_in(src_ref, dst_ref, send_sems, recv_sems, me, devices):
    def finish(k, carry):
        peer = (me + k) % devices
        ship(
            src_ref.at[peer], dst_ref.at[peer], send_sems.at[peer], recv_sems.at[peer], peer
        ).wait()
        return carry

    lax.fori_loop(1, devices, finish, 0)


def kernel(
    devices, capacity, margin, classes,
    z_hbm, coarse_hbm, fine_hbm, parent_hbm, nbr_hbm, seg_hbm,
    w_parent_hbm, w_skip_hbm, taps_hbm, w_cpe_hbm,
    w_qkv_hbm, w_out_hbm, w_up_hbm, w_down_hbm, w_cls_hbm,
    out_ref,
    z_ref, coarse_ref, fine_ref, parent_ref, nbr_ref, seg_ref,
    w_parent_ref, w_skip_ref, taps_ref, w_cpe_ref,
    w_qkv_ref, w_out_ref, w_up_ref, w_down_ref, w_cls_ref,
    pos_ref, got_ref, share_ref, slot_ref, take_ref, par_ref, skip_ref, feat_ref, x_ref, send_ref, recv_ref,
    z_sum_ref, zx_ref, wqv_ref, wk_ref, kx_ref, qh_ref, ql_ref, v_ref, fq_ref, s_ref, m_ref, att_ref,
    logit_ref, back_ref, ret_ref, part_ref, home_ref,
    slot_send, slot_recv, feat_send, feat_recv, back_send, back_recv, side_send, side_recv, load_sem,
):
    me = lax.axis_index(AXES)
    entered = greet(me, devices)
    order = (
        (coarse_hbm, coarse_ref), (w_parent_hbm, w_parent_ref),
        (fine_hbm, fine_ref), (w_skip_hbm, w_skip_ref), (z_hbm, z_ref), (parent_hbm, parent_ref),
        (nbr_hbm, nbr_ref), (taps_hbm, taps_ref), (w_cpe_hbm, w_cpe_ref), (seg_hbm, seg_ref),
        (w_qkv_hbm, w_qkv_ref), (w_out_hbm, w_out_ref),
        (w_up_hbm, w_up_ref), (w_down_hbm, w_down_ref), (w_cls_hbm, w_cls_ref),
    )
    loads = [
        pltpu.make_async_copy(src, dst, load_sem.at[i]) for i, (src, dst) in enumerate(order)
    ]
    for load in loads:
        load.start()
    rows, width = fine_ref.shape
    coarse_rows = coarse_ref.shape[0]
    coarse = par_ref.shape[0]
    total = devices * capacity
    head_dim = width // HEADS
    block = 256
    lanes = 128
    per_group = 4
    gw = per_group * head_dim
    after, before = (me + 1) % devices, (me + devices - 1) % devices

    for load in loads[:2]:
        load.wait()
    par_ref[margin : margin + coarse_rows, :] = gelu(
        layer_norm(dot(coarse_ref[...], w_parent_ref[...]))
    ).astype(BF)
    entered()
    margins = [
        ship(
            par_ref.at[pl.ds(coarse_rows, margin), :], par_ref.at[pl.ds(0, margin), :],
            side_send.at[0], side_recv.at[0], after,
        ),
        ship(
            par_ref.at[pl.ds(margin, margin), :],
            par_ref.at[pl.ds(margin + coarse_rows, margin), :],
            side_send.at[1], side_recv.at[1], before,
        ),
    ]
    for move in margins:
        move.start()

    for load in loads[2:6]:
        load.wait()
    skip_ref[...] = gelu(layer_norm(dot(fine_ref[...], w_skip_ref[...])))

    z = z_ref[...]
    dest = z // rows
    slot = z % rows
    onehot = pick(dest, devices, rows, 0)
    earlier = lax.broadcasted_iota(I32, (rows, rows), 0) < lax.broadcasted_iota(I32, (rows, rows), 1)
    ahead_of = dot(onehot, jnp.where(earlier, 1.0, 0.0).astype(BF))
    rank = jnp.sum(ahead_of * onehot.astype(F32), axis=0, keepdims=True).astype(I32)
    pos = dest * capacity + rank
    pos_ref[...] = pos

    code = slot + 1
    part = lax.broadcasted_iota(I32, (16, rows), 0)
    digits = jnp.where(part == 0, code // 32, jnp.where(part == 1, code % 32, 0))
    digits = digits.astype(F32).astype(BF)
    piece = min(512, total)
    for start in range(0, total, piece):
        got = dot_nt(digits, pick(pos - start, piece, rows, 0)).astype(I32)
        got = got[0:1] * 32 + got[1:2] - 1
        for d in range(piece // capacity):
            slot_ref[start // capacity + d] = got[:, d * capacity : (d + 1) * capacity]
    spread(slot_ref, take_ref, slot_send, slot_recv, me, devices)
    take_ref[me] = slot_ref[me]

    base_row = me * coarse_rows - margin
    for move in margins:
        move.wait()

    def join(i):
        base = i * block
        at = slice(base, base + block)
        chosen = dot(pick(column(parent_ref[:, at] - base_row), block, coarse, 1), par_ref[...])
        feat_ref[base + REACH : base + REACH + block, :] = (chosen + skip_ref[at, :]).astype(BF)

    blocks = rows // block
    edges = [
        ship(
            feat_ref.at[pl.ds(rows, REACH), :], feat_ref.at[pl.ds(0, REACH), :],
            side_send.at[2], side_recv.at[2], after,
        ),
        ship(
            feat_ref.at[pl.ds(REACH, REACH), :], feat_ref.at[pl.ds(REACH + rows, REACH), :],
            side_send.at[3], side_recv.at[3], before,
        ),
    ]
    join(blocks - 1)
    edges[0].start()
    join(0)
    edges[1].start()
    for i in range(1, blocks - 1):
        join(i)

    window = block + 2 * REACH
    for load in loads[6:9]:
        load.wait()

    def conv(i, carry):
        base = pl.multiple_of(i * block, block)
        at = pl.ds(base, block)
        cells = feat_ref[pl.ds(base, window), :]
        offsets = nbr_ref[:, at].T
        here = lax.broadcasted_iota(I32, offsets.shape, 0) + REACH
        source = jnp.where(offsets != REACH + 1, here + offsets, -1)
        middle = nbr_ref.shape[0] // 2
        center = feat_ref[pl.ds(base + REACH, block), :].astype(F32)
        acc = center * taps_ref[middle : middle + 1, :]
        for t in range(nbr_ref.shape[0]):
            if t == middle:
                continue
            acc = acc + dot(pick(source[:, t : t + 1], block, window, 1), cells) * taps_ref[t : t + 1, :]
        out = layer_norm(dot(acc.astype(BF), w_cpe_ref[...]))
        x_ref[at, :] = (center + out).astype(BF)
        return carry

    lax.fori_loop(1, blocks - 1, conv, 0)
    for move in edges:
        move.wait()
    lax.fori_loop(0, 2, lambda i, carry: conv(i * (blocks - 1), carry), 0)

    pos = pos_ref[...]
    per = block // capacity
    shares = devices // per
    stride = 2

    def block_of(j):
        half = shares // stride
        shift = jnp.where(j < half, stride * j + 1, stride * (j - half) + 2)
        return (me // per + shift) % shares

    def pack(j, carry):
        b = block_of(j)
        sent = dot(pick(pos - b * block, block, rows, 0), x_ref[...]).astype(BF)
        send_ref[pl.ds(b * per, per)] = sent.reshape(per, capacity, width)

        def start(k, inner):
            peer = b * per + k

            @pl.when(peer != me)
            def _():
                ship(
                    send_ref.at[peer], recv_ref.at[me], feat_send.at[peer], feat_recv.at[me], peer
                ).start()

            return inner

        lax.fori_loop(0, per, start, 0)
        return carry

    lax.fori_loop(0, shares, pack, 0)
    recv_ref[me] = send_ref[me]

    for load in loads[9:]:
        load.wait()
    bits = (PATCH - 1).bit_length()
    seg = seg_ref[...] - seg_ref[:, 0:1]
    row = lax.broadcasted_iota(I32, (lanes, rows), 0)
    code = ((seg >> (row >> 1)) & 1) ^ (row & 1)
    fq_ref[...] = jnp.where((row < 2 * bits) & (code == 1), 1.0, 0.0).astype(BF)
    lane = lax.broadcasted_iota(I32, (rows, lanes), 1)
    seg_col = jnp.broadcast_to(seg, (lanes, rows)).T
    code = ((seg_col >> (lane >> 1)) & 1) ^ (lane & 1)
    fk = jnp.where((lane < 2 * bits) & (code == 0), -1e30, 0.0).astype(BF)
    for g in range(HEADS // per_group):
        kx_ref[g, :, 2 * gw : 2 * gw + lanes] = fk


    gather_in(slot_ref, take_ref, slot_send, slot_recv, me, devices)
    for d in range(devices):
        got_ref[:, d * capacity : (d + 1) * capacity] = take_ref[d]
    wqv_ref[0:width, :] = w_qkv_ref[:, 0:width].astype(F32).T.astype(BF)
    wqv_ref[width : 2 * width, :] = w_qkv_ref[:, 2 * width :].astype(F32).T.astype(BF)
    for g in range(HEADS // per_group):
        part = w_qkv_ref[:, width + g * gw : width + (g + 1) * gw]
        wk_ref[:, 2 * g * gw : 2 * (g + 1) * gw] = jnp.concatenate([part, part], axis=1)
    z_sum_ref[...] = jnp.zeros_like(z_sum_ref)
    att_ref[...] = jnp.zeros_like(att_ref)
    logit_ref[...] = jnp.zeros_like(logit_ref)
    for d in range(shares):
        share_ref[d] = got_ref[:, d * block : (d + 1) * block]

    def collect(j, carry):
        b = block_of(shares - 1 - j)

        def finish(k, inner):
            peer = b * per + k

            @pl.when(peer != me)
            def _():
                ship(
                    send_ref.at[peer], recv_ref.at[peer], feat_send.at[peer], feat_recv.at[peer], peer
                ).wait()

            return inner

        lax.fori_loop(0, per, finish, 0)
        came = recv_ref[pl.ds(b * per, per)].reshape(block, width)
        z_sum_ref[...] += dot(pick(share_ref[b], rows, block, 0), came)
        return carry

    lax.fori_loop(0, shares, collect, 0)

    z = z_sum_ref[...]
    zx_ref[...] = z.astype(BF)
    normed = layer_norm(z).astype(BF)
    for g in range(0, HEADS // per_group, 2):
        k = dot(normed, wk_ref[:, 2 * g * gw : 2 * (g + 2) * gw]).astype(BF)
        kx_ref[g, :, 0 : 2 * gw] = k[:, : 2 * gw]
        kx_ref[g + 1, :, 0 : 2 * gw] = k[:, 2 * gw :]
    qv = dot_nt(wqv_ref[...], normed)
    q = qv[:width].astype(BF).astype(F32) * (head_dim**-0.5 * math.log2(math.e))
    high = q.astype(BF)
    qh_ref[...] = high
    ql_ref[...] = (q - high.astype(F32)).astype(BF)
    v_ref[...] = qv[width:].astype(BF)

    qb = 256
    units = rows // qb
    ahead = 2
    slots = 4
    span = 512
    row_head = lax.broadcasted_iota(I32, (gw, qb), 0) // head_dim

    def strip(b):
        return pl.ds(pl.multiple_of(b * qb, qb), qb)

    def weights(h, b):
        at = slice((h // per_group) * gw, (h // per_group + 1) * gw)
        mine = row_head == h % per_group
        zero = jnp.zeros((), BF)
        return jnp.concatenate(
            [
                jnp.where(mine, qh_ref[at, strip(b)], zero),
                jnp.where(mine, ql_ref[at, strip(b)], zero),
                fq_ref[:, strip(b)],
            ],
            axis=0,
        )

    def score(h, slot, w, start, top):
        s = dot(kx_ref[h // per_group, start : start + span, :], w)
        s_ref[slot, start : start + span, :] = s
        part = jnp.max(s.reshape(span // 8, 8, qb), axis=0)
        return part if top is None else jnp.maximum(top, part)

    for h in range(ahead):
        w, top = weights(h, 0), None
        for start in range(0, rows, span):
            top = score(h, h % slots, w, start, top)
        m_ref[h % slots] = top

    def tail(b):
        state = {}

        def enter():
            o = lax.dot_general(
                att_ref[:, strip(b)], w_out_ref[...], (((0,), (0,)), ((), ())),
                preferred_element_type=F32,
            ).astype(BF)
            state["x"] = zx_ref[strip(b), :].astype(F32) + o.astype(F32)
            state["n"] = layer_norm(state["x"]).astype(BF)

        def part_of(c):
            at = slice(c * block, (c + 1) * block)
            hidden = gelu(dot(state["n"], w_up_ref[:, at]).astype(BF))
            state["x"] = state["x"] + dot(hidden, w_down_ref[at, :])

        def leave():
            normed = layer_norm(state["x"]).astype(BF)
            logit_ref[0:classes, strip(b)] = dot_nt(w_cls_ref[...], normed)

        chunks = w_up_ref.shape[1] // block
        return [enter] + [functools.partial(part_of, c) for c in range(chunks)] + [leave]

    def step(b, carry):
        work = tail(jnp.maximum(b - 1, 0))
        for h in range(HEADS):
            cur, nxt = h % slots, h + ahead
            later = nxt % HEADS
            w, top = weights(later, jnp.minimum(b + nxt // HEADS, units - 1)), None
            peak = jnp.max(m_ref[cur], axis=0, keepdims=True)
            own = slice(h * head_dim, (h + 1) * head_dim)
            values = jnp.concatenate([v_ref[own, :], jnp.ones((head_dim, rows), BF)], axis=0)
            acc = None
            for start in range(0, rows, span):
                top = score(later, nxt % slots, w, start, top)
                for c in range(start, start + span, block):
                    probs = jnp.exp2(s_ref[cur, c : c + block, :] - peak).astype(BF)
                    part = dot(values[:, c : c + block], probs)
                    acc = part if acc is None else acc + part
            m_ref[nxt % slots] = top
            if h % 2 == 0 and h // 2 < len(work):
                work[h // 2]()
            att = acc[:head_dim] / acc[head_dim : head_dim + 1]
            att_ref[own, strip(b)] = att.astype(BF)
        return carry

    lax.fori_loop(0, units, step, 0)
    for piece_of_work in tail(units - 1):
        piece_of_work()

    logits = logit_ref[...].astype(BF)
    piece = min(512, total // 2)
    peers = devices // 2
    for side in range(2):
        for start in range(side * total // 2, (side + 1) * total // 2, piece):
            got = dot(logits, pick(got_ref[:, start : start + piece], rows, piece, 0)).astype(BF)
            for d in range(piece // capacity):
                at = slice(d * capacity, (d + 1) * capacity)
                back_ref[start // capacity + d] = got[:, at]

        def start_back(k, carry):
            peer = side * peers + (me + k) % peers

            @pl.when(peer != me)
            def _():
                ship(
                    back_ref.at[peer], ret_ref.at[me], back_send.at[peer], back_recv.at[me], peer
                ).start()

            return carry

        lax.fori_loop(0, peers, start_back, 0)
    ret_ref[me] = back_ref[me]

    for side in range(2):

        def finish_back(k, carry):
            peer = side * peers + (me + k) % peers

            @pl.when(peer != me)
            def _():
                ship(
                    back_ref.at[peer], ret_ref.at[peer], back_send.at[peer], back_recv.at[peer], peer
                ).wait()

            return carry

        lax.fori_loop(0, peers, finish_back, 0)
        for d in range(peers):
            part_ref[:, d * capacity : (d + 1) * capacity] = ret_ref[side * peers + d]
        found = dot(part_ref[...], pick(pos_ref[...] - side * (total // 2), total // 2, rows, 0))
        if side == 0:
            home_ref[...] = found
        else:
            home_ref[...] += found

    out_ref[...] = home_ref[0:classes, :]


def local(
    coarse_feats,
    fine_feats,
    parent_index,
    nbr_offset,
    z_position,
    segment_id,
    w_parent,
    w_skip,
    conv_taps,
    w_cpe,
    w_qkv,
    w_out,
    w_up,
    w_down,
    w_cls,
):
    fine_rows, width = fine_feats.shape
    coarse_rows = coarse_feats.shape[0]
    devices = lax.axis_size(AXES)
    capacity = 2 * fine_rows // devices
    total = devices * capacity
    assert fine_rows == PATCH

    margin = coarse_rows // 2
    lanes = 128
    classes = w_cls.shape[0]
    half = -(-classes // 16) * 16
    pair = pltpu.SemaphoreType.DMA((devices,))
    side = pltpu.SemaphoreType.DMA((4,))
    operands = (
        z_position.reshape(1, fine_rows), coarse_feats, fine_feats,
        parent_index.reshape(1, fine_rows), nbr_offset, segment_id.reshape(1, fine_rows),
        w_parent, w_skip, conv_taps, w_cpe, w_qkv, w_out, w_up, w_down, w_cls,
    )
    return pl.pallas_call(
        functools.partial(kernel, devices, capacity, margin, classes),
        out_shape=jax.ShapeDtypeStruct((classes, fine_rows), F32),
        in_specs=[pl.BlockSpec(memory_space=pl.ANY)] * len(operands),
        out_specs=VM,
        scratch_shapes=[
            *[pltpu.VMEM(a.shape, a.dtype) for a in operands],
            pltpu.VMEM((1, fine_rows), I32),
            pltpu.VMEM((1, total), I32),
            pltpu.VMEM((total // 256, 1, 256), I32),
            pltpu.VMEM((devices, 1, capacity), I32),
            pltpu.VMEM((devices, 1, capacity), I32),
            pltpu.VMEM((coarse_rows + 2 * margin, width), BF),
            pltpu.VMEM((fine_rows, width), F32),
            pltpu.VMEM((fine_rows + 2 * REACH, width), BF),
            pltpu.VMEM((fine_rows, width), BF),
            pltpu.VMEM((devices, capacity, width), BF),
            pltpu.VMEM((devices, capacity, width), BF),
            pltpu.VMEM((fine_rows, width), F32),
            pltpu.VMEM((fine_rows, width), BF),
            pltpu.VMEM((2 * width, width), BF),
            pltpu.VMEM((width, 2 * width), BF),
            pltpu.VMEM((HEADS // 4, fine_rows, width // 2 + lanes), BF),
            pltpu.VMEM((width, fine_rows), BF),
            pltpu.VMEM((width, fine_rows), BF),
            pltpu.VMEM((width, fine_rows), BF),
            pltpu.VMEM((lanes, fine_rows), BF),
            pltpu.VMEM((4, fine_rows, 256), F32),
            pltpu.VMEM((4, 8, 256), F32),
            pltpu.VMEM((width, fine_rows), BF),
            pltpu.VMEM((half, fine_rows), F32),
            pltpu.VMEM((devices, half, capacity), BF),
            pltpu.VMEM((devices, half, capacity), BF),
            pltpu.VMEM((half, total // 2), BF),
            pltpu.VMEM((half, fine_rows), F32),
            pair, pair, pair, pair, pair, pair, side, side,
            pltpu.SemaphoreType.DMA((len(operands),)),
        ],
        compiler_params=pltpu.CompilerParams(
            collective_id=0, has_side_effects=True, vmem_limit_bytes=60 * 2**20
        ),
    )(*operands)


def solution(mesh):
    rows = P(AXES, None)
    flat = P(AXES)
    placed = (rows, rows, flat, P(None, AXES), flat, flat) + (P(),) * 9
    return jax.shard_map(
        local, mesh=mesh, in_specs=placed, out_specs=P(None, AXES), check_vma=False
    )
```

```python
import functools
import math

import jax
import jax.numpy as jnp
from jax import lax
from jax.experimental import pallas as pl
from jax.experimental.pallas import tpu as pltpu
from jax.sharding import PartitionSpec as P

HEADS = 16
PATCH = 1024
REACH = 256
AXES = ("row", "col")
BF = jnp.bfloat16
F32 = jnp.float32
I32 = jnp.int32
I16 = jnp.int16
VM = pl.BlockSpec(memory_space=pltpu.VMEM)


def dot(a, b):
    return jnp.dot(a, b, preferred_element_type=F32)


def dot_nt(a, b):
    return lax.dot_general(a, b, (((1,), (1,)), ((), ())), preferred_element_type=F32)


def layer_norm(values):
    center = values - jnp.mean(values, axis=-1, keepdims=True)
    spread = jnp.mean(center * center, axis=-1, keepdims=True)
    return center * lax.rsqrt(spread + 1e-05)


def gelu(x):
    half = 0.5 * x
    return half + half * jnp.tanh(x * (0.7978845608028654 + 0.035677408136300125 * (x * x)))


def pick(index, rows, cols, dim):
    grid = lax.broadcasted_iota(I16, (rows, cols), dim)
    if dim == 0:
        index = jnp.broadcast_to(index, (16, cols)).astype(I16)[0:1]
    else:
        index = jnp.broadcast_to(index, (rows, 128)).astype(I16)
        index = jnp.concatenate([index] * (cols // 128), axis=1)
    return jnp.where(grid == index, jnp.ones((), BF), jnp.zeros((), BF))


def column(row):
    return jnp.broadcast_to(row, (128, row.shape[1])).T[:, :1]


def place(device):
    inner = lax.axis_size("col")
    return (device // inner, device % inner)


def greet(me, devices):
    barrier = pltpu.get_barrier_semaphore()

    def signal(k, carry):
        pl.semaphore_signal(
            barrier, inc=1, device_id=place((me + k) % devices),
            device_id_type=pl.DeviceIdType.MESH,
        )
        return carry

    lax.fori_loop(1, devices, signal, 0)
    return lambda: pl.semaphore_wait(barrier, devices - 1)


def ship(src, dst, send_sem, recv_sem, device):
    return pltpu.make_async_remote_copy(
        src_ref=src, dst_ref=dst, send_sem=send_sem, recv_sem=recv_sem,
        device_id=place(device), device_id_type=pl.DeviceIdType.MESH,
    )


def spread(src_ref, dst_ref, send_sems, recv_sems, me, devices):
    def start(k, carry):
        peer = (me + k) % devices
        ship(
            src_ref.at[peer], dst_ref.at[me], send_sems.at[peer], recv_sems.at[me], peer
        ).start()
        return carry

    lax.fori_loop(1, devices, start, 0)


def gather_in(src_ref, dst_ref, send_sems, recv_sems, me, devices):
    def finish(k, carry):
        peer = (me + k) % devices
        ship(
            src_ref.at[peer], dst_ref.at[peer], send_sems.at[peer], recv_sems.at[peer], peer
        ).wait()
        return carry

    lax.fori_loop(1, devices, finish, 0)


def kernel(
    devices, capacity, margin, classes,
    z_hbm, coarse_hbm, fine_hbm, parent_hbm, nbr_hbm, seg_hbm,
    w_parent_hbm, w_skip_hbm, taps_hbm, w_cpe_hbm,
    w_qkv_hbm, w_out_hbm, w_up_hbm, w_down_hbm, w_cls_hbm,
    out_ref,
    z_ref, coarse_ref, fine_ref, parent_ref, nbr_ref, seg_ref,
    w_parent_ref, w_skip_ref, taps_ref, w_cpe_ref,
    w_qkv_ref, w_out_ref, w_up_ref, w_down_ref, w_cls_ref,
    pos_ref, got_ref, share_ref, slot_ref, take_ref, par_ref, skip_ref, feat_ref, x_ref, send_ref, recv_ref,
    z_sum_ref, zx_ref, wqv_ref, wk_ref, kx_ref, qh_ref, ql_ref, v_ref, fq_ref, s_ref, m_ref, att_ref,
    logit_ref, back_ref, ret_ref, part_ref, home_ref,
    slot_send, slot_recv, feat_send, feat_recv, back_send, back_recv, side_send, side_recv, load_sem,
):
    me = lax.axis_index(AXES)
    entered = greet(me, devices)
    order = (
        (coarse_hbm, coarse_ref), (w_parent_hbm, w_parent_ref),
        (fine_hbm, fine_ref), (w_skip_hbm, w_skip_ref), (z_hbm, z_ref), (parent_hbm, parent_ref),
        (nbr_hbm, nbr_ref), (taps_hbm, taps_ref), (w_cpe_hbm, w_cpe_ref), (seg_hbm, seg_ref),
        (w_qkv_hbm, w_qkv_ref), (w_out_hbm, w_out_ref),
        (w_up_hbm, w_up_ref), (w_down_hbm, w_down_ref), (w_cls_hbm, w_cls_ref),
    )
    loads = [
        pltpu.make_async_copy(src, dst, load_sem.at[i]) for i, (src, dst) in enumerate(order)
    ]
    for load in loads:
        load.start()
    rows, width = fine_ref.shape
    coarse_rows = coarse_ref.shape[0]
    coarse = par_ref.shape[0]
    total = devices * capacity
    head_dim = width // HEADS
    block = 256
    lanes = 128
    per_group = 4
    gw = per_group * head_dim
    after, before = (me + 1) % devices, (me + devices - 1) % devices

    for load in loads[:2]:
        load.wait()
    par_ref[2 * margin :, :] = gelu(
        layer_norm(dot(coarse_ref[...], w_parent_ref[...]))
    ).astype(BF)
    entered()
    margins = [
        ship(
            par_ref.at[pl.ds(margin + coarse_rows, margin), :],
            par_ref.at[pl.ds(margin, margin), :],
            side_send.at[0], side_recv.at[0], after,
        ),
        ship(
            par_ref.at[pl.ds(2 * margin, margin), :], par_ref.at[pl.ds(0, margin), :],
            side_send.at[1], side_recv.at[1], before,
        ),
    ]
    for move in margins:
        move.start()

    for load in loads[2:6]:
        load.wait()
    skip_ref[...] = gelu(layer_norm(dot(fine_ref[...], w_skip_ref[...])))

    z = z_ref[...]
    dest = z // rows
    slot = z % rows
    onehot = pick(dest, devices, rows, 0)
    earlier = lax.broadcasted_iota(I32, (rows, rows), 0) < lax.broadcasted_iota(I32, (rows, rows), 1)
    ahead_of = dot(onehot, jnp.where(earlier, 1.0, 0.0).astype(BF))
    rank = jnp.sum(ahead_of * onehot.astype(F32), axis=0, keepdims=True).astype(I32)
    pos = dest * capacity + rank
    pos_ref[...] = pos

    code = slot + 1
    part = lax.broadcasted_iota(I32, (16, rows), 0)
    digits = jnp.where(part == 0, code // 32, jnp.where(part == 1, code % 32, 0))
    digits = digits.astype(F32).astype(BF)
    piece = min(512, total)
    for start in range(0, total, piece):
        got = dot_nt(digits, pick(pos - start, piece, rows, 0)).astype(I32)
        got = got[0:1] * 32 + got[1:2] - 1
        for d in range(piece // capacity):
            slot_ref[start // capacity + d] = got[:, d * capacity : (d + 1) * capacity]
    spread(slot_ref, take_ref, slot_send, slot_recv, me, devices)
    take_ref[me] = slot_ref[me]

    source_row = parent_ref[...] - (me * coarse_rows - 2 * margin)
    source_row = jnp.where(source_row < coarse, source_row, source_row - coarse)

    def chosen(at, first, count):
        hot = pick(column(source_row[:, at] - first), block, count, 1)
        return dot(hot, par_ref[first : first + count, :])

    for start in range(0, rows, block):
        at = slice(start, start + block)
        skip_ref[at, :] += chosen(at, 2 * margin, coarse_rows)
    for move in margins:
        move.wait()

    def join(i):
        base = i * block
        at = slice(base, base + block)
        joined = (skip_ref[at, :] + chosen(at, 0, 2 * margin)).astype(BF)
        feat_ref[base + REACH : base + REACH + block, :] = joined

    blocks = rows // block
    edges = [
        ship(
            feat_ref.at[pl.ds(rows, REACH), :], feat_ref.at[pl.ds(0, REACH), :],
            side_send.at[2], side_recv.at[2], after,
        ),
        ship(
            feat_ref.at[pl.ds(REACH, REACH), :], feat_ref.at[pl.ds(REACH + rows, REACH), :],
            side_send.at[3], side_recv.at[3], before,
        ),
    ]
    join(blocks - 1)
    edges[0].start()
    join(0)
    edges[1].start()
    for i in range(1, blocks - 1):
        join(i)

    window = block + 2 * REACH
    for load in loads[6:9]:
        load.wait()

    def conv(i, carry):
        base = pl.multiple_of(i * block, block)
        at = pl.ds(base, block)
        cells = feat_ref[pl.ds(base, window), :]
        offsets = nbr_ref[:, at].T
        here = lax.broadcasted_iota(I32, offsets.shape, 0) + REACH
        source = jnp.where(offsets != REACH + 1, here + offsets, -1)
        middle = nbr_ref.shape[0] // 2
        center = feat_ref[pl.ds(base + REACH, block), :].astype(F32)
        acc = center * taps_ref[middle : middle + 1, :]
        for t in range(nbr_ref.shape[0]):
            if t == middle:
                continue
            acc = acc + dot(pick(source[:, t : t + 1], block, window, 1), cells) * taps_ref[t : t + 1, :]
        out = layer_norm(dot(acc.astype(BF), w_cpe_ref[...]))
        x_ref[at, :] = (center + out).astype(BF)
        return carry

    lax.fori_loop(1, blocks - 1, conv, 0)
    for move in edges:
        move.wait()
    lax.fori_loop(0, 2, lambda i, carry: conv(i * (blocks - 1), carry), 0)

    pos = pos_ref[...]
    per = block // capacity
    shares = devices // per
    stride = 2

    def block_of(j):
        half = shares // stride
        shift = jnp.where(j < half, stride * j + 1, stride * (j - half) + 2)
        return (me // per + shift) % shares

    def pack(j, carry):
        b = block_of(j)
        sent = dot(pick(pos - b * block, block, rows, 0), x_ref[...]).astype(BF)
        send_ref[pl.ds(b * per, per)] = sent.reshape(per, capacity, width)

        def start(k, inner):
            peer = b * per + k

            @pl.when(peer != me)
            def _():
                ship(
                    send_ref.at[peer], recv_ref.at[me], feat_send.at[peer], feat_recv.at[me], peer
                ).start()

            return inner

        lax.fori_loop(0, per, start, 0)
        return carry

    lax.fori_loop(0, shares, pack, 0)
    recv_ref[me] = send_ref[me]

    for load in loads[9:]:
        load.wait()
    bits = (PATCH - 1).bit_length()
    seg = seg_ref[...] - seg_ref[:, 0:1]
    row = lax.broadcasted_iota(I32, (lanes, rows), 0)
    code = ((seg >> (row >> 1)) & 1) ^ (row & 1)
    fq_ref[...] = jnp.where((row < 2 * bits) & (code == 1), 1.0, 0.0).astype(BF)
    lane = lax.broadcasted_iota(I32, (rows, lanes), 1)
    seg_col = jnp.broadcast_to(seg, (lanes, rows)).T
    code = ((seg_col >> (lane >> 1)) & 1) ^ (lane & 1)
    fk = jnp.where((lane < 2 * bits) & (code == 0), -1e30, 0.0).astype(BF)
    for g in range(HEADS // per_group):
        kx_ref[g, :, 2 * gw : 2 * gw + lanes] = fk


    gather_in(slot_ref, take_ref, slot_send, slot_recv, me, devices)
    for d in range(devices):
        got_ref[:, d * capacity : (d + 1) * capacity] = take_ref[d]
    wqv_ref[0:width, :] = w_qkv_ref[:, 0:width].astype(F32).T.astype(BF)
    wqv_ref[width : 2 * width, :] = w_qkv_ref[:, 2 * width :].astype(F32).T.astype(BF)
    for g in range(HEADS // per_group):
        part = w_qkv_ref[:, width + g * gw : width + (g + 1) * gw]
        wk_ref[:, 2 * g * gw : 2 * (g + 1) * gw] = jnp.concatenate([part, part], axis=1)
    z_sum_ref[...] = jnp.zeros_like(z_sum_ref)
    for d in range(shares):
        share_ref[d] = got_ref[:, d * block : (d + 1) * block]

    def collect(j, carry):
        b = block_of(shares - 1 - j)

        def finish(k, inner):
            peer = b * per + k

            @pl.when(peer != me)
            def _():
                ship(
                    send_ref.at[peer], recv_ref.at[peer], feat_send.at[peer], feat_recv.at[peer], peer
                ).wait()

            return inner

        lax.fori_loop(0, per, finish, 0)
        came = recv_ref[pl.ds(b * per, per)].reshape(block, width)
        z_sum_ref[...] += dot(pick(share_ref[b], rows, block, 0), came)
        return carry

    lax.fori_loop(0, shares, collect, 0)

    z = z_sum_ref[...]
    zx_ref[...] = z.astype(BF)
    normed = layer_norm(z).astype(BF)
    for g in range(0, HEADS // per_group, 2):
        k = dot(normed, wk_ref[:, 2 * g * gw : 2 * (g + 2) * gw]).astype(BF)
        kx_ref[g, :, 0 : 2 * gw] = k[:, : 2 * gw]
        kx_ref[g + 1, :, 0 : 2 * gw] = k[:, 2 * gw :]
    qv = dot_nt(wqv_ref[...], normed)
    q = qv[:width].astype(BF).astype(F32) * (head_dim**-0.5 * math.log2(math.e))
    high = q.astype(BF)
    qh_ref[...] = high
    ql_ref[...] = (q - high.astype(F32)).astype(BF)
    v_ref[...] = qv[width:].astype(BF)

    qb = 256
    units = rows // qb
    heads_a_step = 8
    ahead = 2
    slots = 4
    row_head = lax.broadcasted_iota(I32, (gw, qb), 0) // head_dim

    def weights(h, b):
        cols = slice(b * qb, (b + 1) * qb)
        at = pl.ds(pl.multiple_of((h // per_group) * gw, gw), gw)
        mine = row_head == h % per_group
        zero = jnp.zeros((), BF)
        return jnp.concatenate(
            [
                jnp.where(mine, qh_ref[at, cols], zero),
                jnp.where(mine, ql_ref[at, cols], zero),
                fq_ref[:, cols],
            ],
            axis=0,
        )

    span = 512

    def score(h, b, slot, w, start, top):
        s = dot(kx_ref[h // per_group, start : start + span, :], w)
        s_ref[slot, start : start + span, :] = s
        part = jnp.max(s.reshape(span // 8, 8, qb), axis=0)
        return part if top is None else jnp.maximum(top, part)

    for u in range(ahead):
        w, top = weights(u // units, u % units), None
        for start in range(0, rows, span):
            top = score(u // units, u % units, u % slots, w, start, top)
        m_ref[u % slots] = top

    def step(i, carry):
        for u in range(heads_a_step * units):
            h, b, cur = i * heads_a_step + u // units, u % units, u % slots
            nxt = u + ahead
            later = jnp.minimum(i * heads_a_step + nxt // units, HEADS - 1)
            w, top = weights(later, nxt % units), None
            peak = jnp.max(m_ref[cur], axis=0, keepdims=True)
            own = pl.ds(pl.multiple_of(h * head_dim, head_dim), head_dim)
            values = jnp.concatenate([v_ref[own, :], jnp.ones((head_dim, rows), BF)], axis=0)
            acc = None
            for start in range(0, rows, span):
                top = score(later, nxt % units, nxt % slots, w, start, top)
                for c in range(start, start + span, block):
                    probs = jnp.exp2(s_ref[cur, c : c + block, :] - peak).astype(BF)
                    part = dot(values[:, c : c + block], probs)
                    acc = part if acc is None else acc + part
            m_ref[nxt % slots] = top
            att = acc[:head_dim] / acc[head_dim : head_dim + 1]
            att_ref[own, b * qb : (b + 1) * qb] = att.astype(BF)
        return carry

    lax.fori_loop(0, HEADS // heads_a_step, step, 0)

    logit_ref[...] = jnp.zeros_like(logit_ref)
    o = lax.dot_general(
        att_ref[...], w_out_ref[...], (((0,), (0,)), ((), ())), preferred_element_type=F32
    ).astype(BF)
    x_two = zx_ref[...].astype(F32) + o.astype(F32)
    hidden = gelu(dot(layer_norm(x_two).astype(BF), w_up_ref[...]).astype(BF))
    x_three = x_two + dot(hidden, w_down_ref[...])
    logit_ref[0:classes, :] = dot_nt(w_cls_ref[...], layer_norm(x_three).astype(BF))

    logits = logit_ref[...].astype(BF)
    piece = min(512, total // 2)
    peers = devices // 2
    for side in range(2):
        for start in range(side * total // 2, (side + 1) * total // 2, piece):
            got = dot(logits, pick(got_ref[:, start : start + piece], rows, piece, 0)).astype(BF)
            for d in range(piece // capacity):
                at = slice(d * capacity, (d + 1) * capacity)
                back_ref[start // capacity + d] = got[:, at]

        def start_back(k, carry):
            peer = side * peers + (me + k) % peers

            @pl.when(peer != me)
            def _():
                ship(
                    back_ref.at[peer], ret_ref.at[me], back_send.at[peer], back_recv.at[me], peer
                ).start()

            return carry

        lax.fori_loop(0, peers, start_back, 0)
    ret_ref[me] = back_ref[me]

    for side in range(2):

        def finish_back(k, carry):
            peer = side * peers + (me + k) % peers

            @pl.when(peer != me)
            def _():
                ship(
                    back_ref.at[peer], ret_ref.at[peer], back_send.at[peer], back_recv.at[peer], peer
                ).wait()

            return carry

        lax.fori_loop(0, peers, finish_back, 0)
        for d in range(peers):
            part_ref[:, d * capacity : (d + 1) * capacity] = ret_ref[side * peers + d]
        found = dot(part_ref[...], pick(pos_ref[...] - side * (total // 2), total // 2, rows, 0))
        if side == 0:
            home_ref[...] = found
        else:
            home_ref[...] += found

    out_ref[...] = home_ref[0:classes, :]


def local(
    coarse_feats,
    fine_feats,
    parent_index,
    nbr_offset,
    z_position,
    segment_id,
    w_parent,
    w_skip,
    conv_taps,
    w_cpe,
    w_qkv,
    w_out,
    w_up,
    w_down,
    w_cls,
):
    fine_rows, width = fine_feats.shape
    coarse_rows = coarse_feats.shape[0]
    devices = lax.axis_size(AXES)
    capacity = 2 * fine_rows // devices
    total = devices * capacity
    assert fine_rows == PATCH

    margin = coarse_rows // 2
    lanes = 128
    classes = w_cls.shape[0]
    half = -(-classes // 16) * 16
    pair = pltpu.SemaphoreType.DMA((devices,))
    side = pltpu.SemaphoreType.DMA((4,))
    operands = (
        z_position.reshape(1, fine_rows), coarse_feats, fine_feats,
        parent_index.reshape(1, fine_rows), nbr_offset, segment_id.reshape(1, fine_rows),
        w_parent, w_skip, conv_taps, w_cpe, w_qkv, w_out, w_up, w_down, w_cls,
    )
    return pl.pallas_call(
        functools.partial(kernel, devices, capacity, margin, classes),
        out_shape=jax.ShapeDtypeStruct((classes, fine_rows), F32),
        in_specs=[pl.BlockSpec(memory_space=pl.ANY)] * len(operands),
        out_specs=VM,
        scratch_shapes=[
            *[pltpu.VMEM(a.shape, a.dtype) for a in operands],
            pltpu.VMEM((1, fine_rows), I32),
            pltpu.VMEM((1, total), I32),
            pltpu.VMEM((total // 256, 1, 256), I32),
            pltpu.VMEM((devices, 1, capacity), I32),
            pltpu.VMEM((devices, 1, capacity), I32),
            pltpu.VMEM((coarse_rows + 2 * margin, width), BF),
            pltpu.VMEM((fine_rows, width), F32),
            pltpu.VMEM((fine_rows + 2 * REACH, width), BF),
            pltpu.VMEM((fine_rows, width), BF),
            pltpu.VMEM((devices, capacity, width), BF),
            pltpu.VMEM((devices, capacity, width), BF),
            pltpu.VMEM((fine_rows, width), F32),
            pltpu.VMEM((fine_rows, width), BF),
            pltpu.VMEM((2 * width, width), BF),
            pltpu.VMEM((width, 2 * width), BF),
            pltpu.VMEM((HEADS // 4, fine_rows, width // 2 + lanes), BF),
            pltpu.VMEM((width, fine_rows), BF),
            pltpu.VMEM((width, fine_rows), BF),
            pltpu.VMEM((width, fine_rows), BF),
            pltpu.VMEM((lanes, fine_rows), BF),
            pltpu.VMEM((4, fine_rows, 256), F32),
            pltpu.VMEM((4, 8, 256), F32),
            pltpu.VMEM((width, fine_rows), BF),
            pltpu.VMEM((half, fine_rows), F32),
            pltpu.VMEM((devices, half, capacity), BF),
            pltpu.VMEM((devices, half, capacity), BF),
            pltpu.VMEM((half, total // 2), BF),
            pltpu.VMEM((half, fine_rows), F32),
            pair, pair, pair, pair, pair, pair, side, side,
            pltpu.SemaphoreType.DMA((len(operands),)),
        ],
        compiler_params=pltpu.CompilerParams(
            collective_id=0, has_side_effects=True, vmem_limit_bytes=60 * 2**20
        ),
    )(*operands)


def solution(mesh):
    rows = P(AXES, None)
    flat = P(AXES)
    placed = (rows, rows, flat, P(None, AXES), flat, flat) + (P(),) * 9
    return jax.shard_map(
        local, mesh=mesh, in_specs=placed, out_specs=P(None, AXES), check_vma=False
    )
```
